32 devices in a mesh: ctx: 8 (over y, x, core), dp: 4 (over z).
Axes of the slice: x: 2, y: 2, z: 4, core: 2. Of those that a mesh axis runs over, the one named last changes fastest.
Arguments:
- query_rows: bfloat16 [32768, 512], P(('dp', 'ctx')), parts along dimension 0, may hold values from -12 to 12
- key_rows: bfloat16 [32768, 512], P(('dp', 'ctx')), parts along dimension 0, may hold values from -12 to 12
- value_rows: bfloat16 [32768, 512], P(('dp', 'ctx')), parts along dimension 0, may hold values from -12 to 12
Outputs:
- attended: bfloat16 [32768, 512], P(('dp', 'ctx')), parts along dimension 0
The draws below stay inside these ranges and needn't reach their ends.
There are 4 independent parts, one for each index of `dp`. The reference program is written for one: setup_inputs(seed, part) draws one part's arguments, and reference() takes and returns one part's arrays. A program takes and returns all parts, laid end to end along the dimension named above; each array names one. Nothing has to cross between parts.
All inputs are finite; a program needn't handle non-finite values.
Results may differ from the reference program's by a relative error of at most 0.0038.
Values may be sent and summed in bfloat16 or wider, within the bound.
No kernel may reach another device: no remote copies, remote signals or barrier semaphores. Data moves between devices by JAX's collectives and lax.ppermute only.
A program may use at most 128 MiB of HBM per device.

```python
import math
import jax
import jax.numpy as jnp
from jax import lax

HEADS = 4
WIDTH = 512
LEAF = 256
LEVELS = 5
TOK_DEV = 1024
SEQ = 8192
N_CTX = 8


def draw_query_rows(key, part):
    return jnp.clip(2.0 * jax.random.normal(jax.random.fold_in(key, 2), (SEQ, WIDTH)), -8.0, 8.0).astype(jnp.bfloat16)


def draw_key_rows(key, part):
    return jnp.clip(jax.random.normal(jax.random.fold_in(key, 4), (SEQ, WIDTH)), -4.0, 4.0).astype(jnp.bfloat16)


def levels(own_key, extent, cuts, low, high):
    def one(axis_at, parts):
        heights = jax.random.uniform(jax.random.fold_in(jax.random.fold_in(own_key, 6), axis_at), (parts,), jnp.float32, low / len(cuts), high / len(cuts))
        return jnp.repeat(jnp.exp(heights), extent[axis_at] // parts).reshape((-1,) + (1,) * (len(extent) - axis_at - 1))

    factor_of = one(*cuts[0])
    for cut in cuts[1:]:
        factor_of = factor_of * one(*cut)
    return factor_of


def scatter_about(stream_key, extent, width, most, shards=(), kind=jnp.bfloat16):
    drawn = width * jax.random.normal(stream_key, extent, jnp.float32)
    if shards:
        drawn = drawn * levels(stream_key, extent, shards, -0.22, 0.18)
    return jnp.clip(drawn, -most, most).astype(kind)


def setup_inputs(seed: int = 0, part: int = 0) -> dict:
    keys = jax.random.split(jax.random.key(seed), 4)
    part_splits = jax.random.split(jax.random.fold_in(keys[3], part), 4)
    return {
        "query_rows": draw_query_rows(jax.random.fold_in(jax.random.fold_in(keys[3], part), 71), part),
        "key_rows": draw_key_rows(jax.random.fold_in(jax.random.fold_in(keys[3], part), 71), part),
        "value_rows": scatter_about(part_splits[2], (SEQ, WIDTH), 3.0, 12.0, ((0, 8),)),
    }


LOG_TWO = math.log(2.0)

def pool_pairs(stacked):
    widened = lax.optimization_barrier(stacked).astype(jnp.float32)
    paired = widened.reshape(widened.shape[0], widened.shape[1] // 2, 2, widened.shape[2])
    return ((paired[:, :, 0] + paired[:, :, 1]) * 0.5).astype(jnp.bfloat16)

def half_offsets(level_num):
    if level_num == 0:
        return ((-2, -1, 0, 1, 2, 3), (-3, -2, -1, 0, 1, 2))
    return ((-2, 2, 3), (-3, -2, 3))

def attend_level(queries, key_table, base_row, first_token, level_num, limit_halves):
    token_rows, width_all = queries.shape
    head_size = width_all // HEADS
    half_size = LEAF // 2
    span_tokens = half_size * 2 ** level_num
    group_rows = min(span_tokens, token_rows)
    group_count = token_rows // group_rows
    per_block = min(max(1, 512 // group_rows), group_count)
    block_count = group_count // per_block
    pattern = jnp.array(half_offsets(level_num), dtype=jnp.int32)
    offset_count = pattern.shape[1]
    inverse_root = 1.0 / math.sqrt(head_size)

    def take_half(start_row):
        return lax.dynamic_slice_in_dim(key_table, start_row, half_size, 1)

    def one_block(block_index):
        slot_ids = block_index * per_block + jnp.arange(per_block, dtype=jnp.int32)
        group_start = first_token + slot_ids * group_rows
        which_half = group_start // span_tokens
        halves = which_half[:, None] + pattern[which_half % 2]
        is_valid = (halves >= 0) & (halves < limit_halves)
        start_rows = (halves * half_size - base_row).astype(jnp.int32)
        picked = jax.vmap(jax.vmap(take_half))(start_rows)
        key_block = picked[:, :, 0].reshape(per_block, offset_count * half_size, HEADS, head_size)
        value_block = picked[:, :, 1].reshape(per_block, offset_count * half_size, HEADS, head_size)
        query_block = lax.dynamic_slice_in_dim(queries, block_index * per_block * group_rows, per_block * group_rows, 0)
        query_block = query_block.reshape(per_block, group_rows, HEADS, head_size)
        scores = jnp.einsum('gqhd,gkhd->ghqk', query_block.astype(jnp.float32), key_block.astype(jnp.float32), preferred_element_type=jnp.float32)
        key_valid = jnp.repeat(is_valid, half_size, axis=1)[:, None, None, :]
        masked = jnp.where(key_valid, scores * inverse_root + level_num * LOG_TWO, -jnp.inf)
        level_peak = lax.optimization_barrier(jnp.max(masked, axis=-1))
        safe_peak = jnp.where(jnp.isfinite(level_peak), level_peak, 0.0)
        weights = jnp.exp(masked - safe_peak[..., None])
        totals = lax.optimization_barrier(jnp.sum(weights, axis=-1))
        rounded = weights.astype(jnp.bfloat16)
        numerator = jnp.einsum('ghqk,gkhd->gqhd', rounded.astype(jnp.float32), value_block.astype(jnp.float32), preferred_element_type=jnp.float32)
        peak_rows = jnp.transpose(level_peak, (0, 2, 1)).reshape(per_block * group_rows, HEADS)
        total_rows = jnp.transpose(totals, (0, 2, 1)).reshape(per_block * group_rows, HEADS)
        return (peak_rows, total_rows, numerator.reshape(per_block * group_rows, HEADS, head_size))
    peak_rows, total_rows, numer_rows = lax.map(one_block, jnp.arange(block_count, dtype=jnp.int32))
    return (peak_rows.reshape(token_rows, HEADS), total_rows.reshape(token_rows, HEADS), numer_rows.reshape(token_rows, HEADS, head_size))

def combine_levels(level_stats, token_rows, width_all):
    overall = level_stats[0][0]
    for entry in level_stats[1:]:
        overall = jnp.maximum(overall, entry[0])
    numerator = jnp.zeros(level_stats[0][2].shape, jnp.float32)
    denominator = jnp.zeros(overall.shape, jnp.float32)
    for level_peak, totals, partial_value in level_stats:
        factor = jnp.exp(level_peak - overall)
        numerator = numerator + factor[:, :, None] * partial_value
        denominator = denominator + factor * totals
    return (numerator / denominator[:, :, None]).reshape(token_rows, width_all).astype(jnp.bfloat16)

def reference(query_rows, key_rows, value_rows):
    seq_rows, width_all = query_rows.shape
    half_size = LEAF // 2
    tables = [jnp.stack([key_rows, value_rows])]
    for level_num in range(1, LEVELS):
        tables.append(pool_pairs(tables[-1]))

    def one_slab(slab_index):
        first_token = slab_index * TOK_DEV
        slab_rows = lax.dynamic_slice_in_dim(query_rows, first_token, TOK_DEV, 0)
        level_stats = []
        for level_num in range(LEVELS):
            limit_halves = seq_rows // (2 ** level_num * half_size)
            level_stats.append(attend_level(slab_rows, tables[level_num], 0, first_token, level_num, limit_halves))
        return combine_levels(level_stats, TOK_DEV, width_all)
    slabs = lax.map(one_slab, jnp.arange(N_CTX, dtype=jnp.int32))
    return slabs.reshape(seq_rows, width_all)
```

```python
import functools
import math

import jax
import jax.numpy as jnp
from jax import lax
from jax.experimental import pallas as pl
from jax.experimental.pallas import tpu as pltpu
from jax.sharding import PartitionSpec as P

HEADS = 4
LEAF = 256
LEVELS = 5
HALF = LEAF // 2
BLOCKS = 4
RIM_ROWS = 576
TABLE_ROWS = 896
L1_AT = 256
L2_AT = 640
FAR_ROWS = 192
HIDDEN = -1e30


def pooled(x):
    rows = x.shape[0]
    parts = []
    start = 0
    while start < rows:
        step = 256 if rows - start >= 256 else 128
        low = lax.broadcasted_iota(jnp.int32, (step // 2, step), 0) * 2
        col = lax.broadcasted_iota(jnp.int32, (step // 2, step), 1)
        pick = jnp.where((col == low) | (col == low + 1), 0.5, 0.0).astype(jnp.bfloat16)
        parts.append(
            jnp.dot(pick, x[start : start + step], preferred_element_type=jnp.float32).astype(
                jnp.bfloat16
            )
        )
        start += step
    return jnp.concatenate(parts, axis=0) if len(parts) > 1 else parts[0]


def pool_kernel(dev_ref, k_ref, v_ref, x1_ref, i1_ref, x2_ref, y_ref, l1_ref):
    odd = dev_ref[0] % 2 == 1
    width = k_ref.shape[1]
    for side, src in enumerate((k_ref, v_ref)):
        lanes = slice(side * width, (side + 1) * width)
        l0 = src
        l1 = pooled(src[...])
        l2 = pooled(l1)
        l3 = pooled(l2)
        l4 = pooled(l3)
        l1_ref[:, lanes] = l1
        y_ref[0:128, lanes] = l3
        y_ref[128:192, lanes] = l4
        i1_ref[L2_AT:TABLE_ROWS, lanes] = l2

        @pl.when(odd)
        def _():
            x1_ref[0:256, lanes] = l0[768:1024, :]
            x1_ref[256:384, lanes] = l1[256:384]
            x1_ref[384:512, lanes] = l2[0:128]
            x1_ref[512:576, lanes] = l2[0:64]
            i1_ref[0:256, lanes] = l0[0:256, :]
            i1_ref[L1_AT:L2_AT, lanes] = l1[0:384]
            x2_ref[0:128, lanes] = l2[0:128]
            x2_ref[128:192, lanes] = l3[64:128]

        @pl.when(jnp.logical_not(odd))
        def _():
            x1_ref[0:256, lanes] = l0[0:256, :]
            x1_ref[256:512, lanes] = l1[128:384]
            x1_ref[512:576, lanes] = l2[192:256]
            i1_ref[0:256, lanes] = l0[768:1024, :]
            i1_ref[L1_AT : L1_AT + 256, lanes] = l1[256:512]
            i1_ref[L1_AT + 256 : L2_AT, lanes] = l1[0:128]
            x2_ref[0:128, lanes] = l3
            x2_ref[128:192, lanes] = l3[64:128]


def share_kernel(dev_ref, x1_ref, x2_ref, *refs):
    y_refs, (xt_ref, i2_ref, own_ref) = refs[:-3], refs[-3:]
    odd = dev_ref[0] % 2 == 1
    xt_ref[0:256, :] = x1_ref[0:256, :]
    for slot, y_ref in enumerate(y_refs):
        i2_ref[384 + 64 * slot : 448 + 64 * slot, :] = y_ref[128:192, :]
        own_ref[128 + 64 * slot : 192 + 64 * slot, :] = y_ref[128:192, :]

    @pl.when(odd)
    def _():
        l1 = jnp.concatenate([pooled(x1_ref[0:256, :]), x1_ref[256:512, :]], axis=0)
        l2 = jnp.concatenate([pooled(l1), x1_ref[512:576, :]], axis=0)
        xt_ref[L1_AT:L2_AT, :] = l1
        xt_ref[L2_AT:TABLE_ROWS, :] = l2
        i2_ref[0:128, :] = l2[0:128]
        i2_ref[128:256, :] = pooled(l2)
        i2_ref[256:384, :] = x2_ref[0:128, :]
        own_ref[0:128, :] = x2_ref[0:128, :]

    @pl.when(jnp.logical_not(odd))
    def _():
        l1 = jnp.concatenate([x1_ref[256:384, :], pooled(x1_ref[0:256, :])], axis=0)
        l2 = jnp.concatenate([x1_ref[384:512, :], pooled(l1)], axis=0)
        xt_ref[L1_AT : L1_AT + 256, :] = l1
        xt_ref[L1_AT + 256 : L2_AT, :] = l1[0:128]
        xt_ref[L2_AT:TABLE_ROWS, :] = l2
        i2_ref[0:128, :] = x2_ref[0:128, :]
        i2_ref[128:256, :] = pooled(l2)
        i2_ref[256:384, :] = y_refs[0][0:128, :]
        own_ref[0:64, :] = pooled(x2_ref[0:128, :])
        own_ref[64:128, :] = x2_ref[128:192, :]


def attend(query, segments, scale, before):
    rows = query.shape[0]
    scores = []
    peak = None
    for k_ref, _, start, count, offset in segments:
        score = lax.dot_general(
            query,
            k_ref[start : start + count, :],
            (((1,), (1,)), ((), ())),
            preferred_element_type=jnp.float32,
        )
        scores.append(score)
        top = score[:, 0:128]
        for col in range(128, count, 128):
            top = jnp.maximum(top, score[:, col : col + 128])
        if count < 128:
            top = jnp.max(score, axis=1, keepdims=True)
        top = top * scale + offset
        if top.shape[1] < 128:
            top = jnp.broadcast_to(top, (rows, 128))
        peak = top if peak is None else jnp.maximum(peak, top)
    peak = jnp.broadcast_to(jnp.max(peak, axis=1, keepdims=True), (rows, 128))
    if before is not None:
        peak = jnp.maximum(peak, before)
    out = None
    for (_, v_ref, start, count, offset), score in zip(segments, scores):
        lifted = peak - offset
        weights = []
        for col in range(0, count, 128):
            piece = score[:, col : min(col + 128, count)]
            weights.append(jnp.exp2(piece * scale - lifted[:, : piece.shape[1]]))
        weight = jnp.concatenate(weights, axis=1) if len(weights) > 1 else weights[0]
        table = jnp.concatenate(
            [v_ref[start : start + count, :], jnp.ones((count, 128), jnp.bfloat16)], axis=1
        )
        part = jnp.dot(
            weight.astype(jnp.bfloat16), table, preferred_element_type=jnp.float32
        )
        out = part if out is None else out + part
    return peak, out[:, 0:128], out[:, 128:256]


def base_two_scale(head_size):
    return math.log2(math.e) / math.sqrt(head_size)


def local_kernel(q_ref, k_ref, v_ref, l1k_ref, l1v_ref, acc_ref, peak_ref, total_ref):
    scale = base_two_scale(q_ref.shape[1])
    own = {0: ((256, 256),), 1: (), 2: ((0, 128),), 3: ((0, 256),)}
    for block in range(BLOCKS):
        low, high = max(block - 1, 0), min(block + 2, BLOCKS)
        segments = [(k_ref, v_ref, low * LEAF, (high - low) * LEAF, 0.0)]
        for start, count in own[block]:
            segments.append((l1k_ref, l1v_ref, start, count, 1.0))
        here = slice(block * LEAF, (block + 1) * LEAF)
        peak, acc, total = attend(q_ref[here, :], segments, scale, None)
        acc_ref[here, :] = acc
        peak_ref[here, :] = peak
        total_ref[here, :] = total


def remote_kernel(flow_spans, count, dev_ref, q_ref, *refs):
    (xtk, xtv, i1k, i1v, i2k, i2v, ownk, ownv, acc_ref, peak_ref, total_ref, out_ref) = refs
    scale = base_two_scale(q_ref.shape[1])
    me = dev_ref[0]
    chip = me // 2
    chips = count // 2

    def offset(level, valid):
        return jnp.where(valid, float(level), HIDDEN).astype(jnp.float32)

    left, right = me >= 1, me < count - 1
    flows = []
    for shifts in flow_spans:
        valid = False
        for shift in shifts:
            source = chip - shift // 2
            here = (source >= 0) & (source < chips)
            if shift == -4:
                here = here & (chip % 2 == 0)
            if shift == 6:
                here = here & (chip % 2 == 1)
            valid = here | valid
        flows.append(valid)

    def run(odd, lk, lv, rk, rv):
        a_ok = (me - 2 >= 0) if odd else (me + 2 < count)
        b_ok = (me + 3 < count) if odd else (me - 2 >= 0)
        c_ok = (me - 3 >= 0) if odd else (me + 3 < count)
        coarse = [
            (i2k, i2v, 128, 128, offset(3, a_ok)),
            (i2k, i2v, 256, 128, offset(3, b_ok)),
            (ownk, ownv, 0, 128, offset(3, c_ok)),
        ]
        for slot, valid in enumerate(flows):
            coarse.append((i2k, i2v, 384 + 64 * slot, 64, offset(4, valid)))
            coarse.append((ownk, ownv, 128 + 64 * slot, 64, offset(4, valid)))
        second = (
            [(lk, lv, L2_AT, 128, offset(2, left)), (rk, rv, L2_AT, 256, offset(2, right))],
            [(lk, lv, L2_AT, 256, offset(2, left)), (i2k, i2v, 0, 128, offset(2, me + 2 < count))],
        )
        edges = (
            [(lk, lv, 0, 256, offset(0, left)), (lk, lv, L1_AT, 128, offset(1, left))],
            [(lk, lv, L1_AT, 256, offset(1, left)), (rk, rv, L1_AT, 128, offset(1, right))],
            [(rk, rv, L1_AT, 256, offset(1, right))],
            [(rk, rv, 0, 256, offset(0, right)), (rk, rv, L1_AT + 256, 128, offset(1, right))],
        )
        for block in range(BLOCKS):
            here = slice(block * LEAF, (block + 1) * LEAF)
            segments = edges[block] + second[block // 2] + coarse
            before = peak_ref[here, :]
            peak, acc, total = attend(q_ref[here, :], segments, scale, before)
            factor = jnp.exp2(before - peak)
            acc = acc_ref[here, :] * factor + acc
            total = total_ref[here, :] * factor + total
            out_ref[here, :] = (acc / total).astype(out_ref.dtype)

    @pl.when(me % 2 == 1)
    def _():
        run(True, i1k, i1v, xtk, xtv)

    @pl.when(me % 2 == 0)
    def _():
        run(False, xtk, xtv, i1k, i1v)


def flow_pairs(shifts, count):
    pairs = []
    for shift in shifts:
        for source in range(count):
            target = source + shift
            if 0 <= target < count and not (shift == 6 and target // 2 % 2 == 0):
                pairs.append((source, target))
    return pairs


def far_flows(count):
    spans = []
    for low, high in ((-4, 4), (-6, 6)):
        pairs = flow_pairs((low, high), count)
        unique = len({s for s, _ in pairs}) == len(pairs) == len({t for _, t in pairs})
        spans.extend([(low, high)] if unique else [(low,), (high,)])
    return tuple(spans)


def on_device(query_rows, key_rows, value_rows):
    token_rows, width = query_rows.shape
    head_size = width // HEADS
    count = lax.axis_size("ctx")
    me = lax.axis_index("ctx").astype(jnp.int32).reshape(1)
    dtype = key_rows.dtype

    def shape(rows, columns=2 * width, kind=dtype):
        return jax.ShapeDtypeStruct((rows, columns), kind)

    smem = pl.BlockSpec(memory_space=pltpu.SMEM)
    vmem = pl.BlockSpec(memory_space=pltpu.VMEM)
    params = pltpu.CompilerParams(vmem_limit_bytes=56 << 20)

    x1s, i1s, x2s, ys, l1 = pl.pallas_call(
        pool_kernel,
        name="pool",
        out_shape=[
            shape(RIM_ROWS), shape(TABLE_ROWS), shape(FAR_ROWS), shape(192), shape(token_rows // 2)
        ],
        in_specs=[smem, vmem, vmem],
        out_specs=[vmem] * 5,
        compiler_params=params,
    )(me, key_rows, value_rows)

    near = range(1, count - 1, 2)
    x1r = lax.ppermute(
        x1s, "ctx", [(i, i + 1) for i in near] + [(i + 1, i) for i in near]
    )
    x2r = lax.ppermute(
        x2s,
        "ctx",
        [(i, i + 3) for i in range(0, count - 3, 2)] + [(i, i - 3) for i in range(3, count, 2)],
    )
    flow_spans = far_flows(count)
    yrs = [lax.ppermute(ys, "ctx", flow_pairs(shifts, count)) for shifts in flow_spans]
    mates = [(i, i ^ 1) for i in range(count)]
    i1r = lax.ppermute(i1s, "ctx", mates)

    def head(rows, base=0):
        return pl.BlockSpec((rows, head_size), lambda h, *_: (0, base + h))

    acc, peak, total = pl.pallas_call(
        local_kernel,
        name="local",
        grid=(HEADS,),
        out_shape=[shape(token_rows, width, jnp.float32)] * 3,
        in_specs=[head(token_rows)] * 3 + [head(token_rows // 2), head(token_rows // 2, HEADS)],
        out_specs=[head(token_rows)] * 3,
        compiler_params=params,
    )(query_rows, key_rows, value_rows, l1, l1)

    share_rows, own_rows = 384 + 64 * len(yrs), 128 + 64 * len(yrs)
    xt, i2s, own = pl.pallas_call(
        share_kernel,
        name="share",
        out_shape=[shape(TABLE_ROWS), shape(share_rows), shape(own_rows)],
        in_specs=[smem] + [vmem] * (2 + len(yrs)),
        out_specs=[vmem] * 3,
        compiler_params=params,
    )(me, x1r, x2r, *yrs)
    i2r = lax.ppermute(i2s, "ctx", mates)

    tables = []
    specs = []
    for table in (xt, i1r, i2r, own):
        tables += [table, table]
        specs += [head(table.shape[0]), head(table.shape[0], HEADS)]
    return pl.pallas_call(
        functools.partial(remote_kernel, flow_spans, count),
        name="remote",
        grid=(HEADS,),
        out_shape=shape(token_rows, width),
        in_specs=[smem, head(token_rows)] + specs + [head(token_rows)] * 3,
        out_specs=head(token_rows),
        compiler_params=params,
    )(me, query_rows, *tables, acc, peak, total)


def solution(mesh):
    spec = P(("dp", "ctx"), None)
    return jax.shard_map(
        on_device, mesh=mesh, in_specs=(spec, spec, spec), out_specs=spec, check_vma=False
    )
```

```python
import functools
import math

import jax
import jax.numpy as jnp
import ml_dtypes
import numpy as np
from jax import lax
from jax.experimental import pallas as pl
from jax.experimental.pallas import tpu as pltpu
from jax.sharding import PartitionSpec as P

HEADS = 4
LEAF = 256
LEVELS = 5
HALF = LEAF // 2
BLOCKS = 4
RIM_ROWS = 576
TABLE_ROWS = 896
L1_AT = 256
L2_AT = 640
FAR_ROWS = 192
HIDDEN = -1e30


def pooled(x):
    rows = x.shape[0]
    parts = []
    start = 0
    while start < rows:
        step = 256 if rows - start >= 256 else 128
        low = lax.broadcasted_iota(jnp.int32, (step // 2, step), 0) * 2
        col = lax.broadcasted_iota(jnp.int32, (step // 2, step), 1)
        pick = jnp.where((col == low) | (col == low + 1), 0.5, 0.0).astype(jnp.bfloat16)
        parts.append(
            jnp.dot(pick, x[start : start + step], preferred_element_type=jnp.float32).astype(
                jnp.bfloat16
            )
        )
        start += step
    return jnp.concatenate(parts, axis=0) if len(parts) > 1 else parts[0]


def pool_kernel(dev_ref, k_ref, v_ref, x1_ref, i1_ref, x2_ref, y_ref, l1_ref):
    odd = dev_ref[0] % 2 == 1
    width = k_ref.shape[1]
    for side, src in enumerate((k_ref, v_ref)):
        lanes = slice(side * width, (side + 1) * width)
        l0 = src
        l1 = pooled(src[...])
        l2 = pooled(l1)
        l3 = pooled(l2)
        l4 = pooled(l3)
        l1_ref[:, lanes] = l1
        y_ref[0:128, lanes] = l3
        y_ref[128:192, lanes] = l4
        i1_ref[L2_AT:TABLE_ROWS, lanes] = l2

        @pl.when(odd)
        def _():
            x1_ref[0:256, lanes] = l0[768:1024, :]
            x1_ref[256:384, lanes] = l1[256:384]
            x1_ref[384:512, lanes] = l2[0:128]
            x1_ref[512:576, lanes] = l2[0:64]
            i1_ref[0:256, lanes] = l0[0:256, :]
            i1_ref[L1_AT:L2_AT, lanes] = l1[0:384]
            x2_ref[0:128, lanes] = l2[0:128]
            x2_ref[128:192, lanes] = l3[64:128]

        @pl.when(jnp.logical_not(odd))
        def _():
            x1_ref[0:256, lanes] = l0[0:256, :]
            x1_ref[256:512, lanes] = l1[128:384]
            x1_ref[512:576, lanes] = l2[192:256]
            i1_ref[0:256, lanes] = l0[768:1024, :]
            i1_ref[L1_AT : L1_AT + 256, lanes] = l1[256:512]
            i1_ref[L1_AT + 256 : L2_AT, lanes] = l1[0:128]
            x2_ref[0:128, lanes] = l3
            x2_ref[128:192, lanes] = l3[64:128]


def share_kernel(dev_ref, x1_ref, x2_ref, *refs):
    y_refs, (xt_ref, i2_ref, own_ref) = refs[:-3], refs[-3:]
    odd = dev_ref[0] % 2 == 1
    xt_ref[0:256, :] = x1_ref[0:256, :]
    for slot, y_ref in enumerate(y_refs):
        i2_ref[384 + 64 * slot : 448 + 64 * slot, :] = y_ref[128:192, :]
        own_ref[128 + 64 * slot : 192 + 64 * slot, :] = y_ref[128:192, :]

    @pl.when(odd)
    def _():
        l1 = jnp.concatenate([pooled(x1_ref[0:256, :]), x1_ref[256:512, :]], axis=0)
        l2 = jnp.concatenate([pooled(l1), x1_ref[512:576, :]], axis=0)
        xt_ref[L1_AT:L2_AT, :] = l1
        xt_ref[L2_AT:TABLE_ROWS, :] = l2
        i2_ref[0:128, :] = l2[0:128]
        i2_ref[128:256, :] = pooled(l2)
        i2_ref[256:384, :] = x2_ref[0:128, :]
        own_ref[0:128, :] = x2_ref[0:128, :]

    @pl.when(jnp.logical_not(odd))
    def _():
        l1 = jnp.concatenate([x1_ref[256:384, :], pooled(x1_ref[0:256, :])], axis=0)
        l2 = jnp.concatenate([x1_ref[384:512, :], pooled(l1)], axis=0)
        xt_ref[L1_AT : L1_AT + 256, :] = l1
        xt_ref[L1_AT + 256 : L2_AT, :] = l1[0:128]
        xt_ref[L2_AT:TABLE_ROWS, :] = l2
        i2_ref[0:128, :] = x2_ref[0:128, :]
        i2_ref[128:256, :] = pooled(l2)
        i2_ref[256:384, :] = y_refs[0][0:128, :]
        own_ref[0:64, :] = pooled(x2_ref[0:128, :])
        own_ref[64:128, :] = x2_ref[128:192, :]


def offset_lanes(level, valid, scale):
    terms = []
    rest = level / scale
    for _ in range(3):
        term = float(np.float32(rest).astype(ml_dtypes.bfloat16))
        terms.append(term)
        rest -= term
    if valid is not None:
        terms = [jnp.where(valid, t, h) for t, h in zip(terms, (HIDDEN, 0.0, 0.0))]
    lane = lax.broadcasted_iota(jnp.int32, (128, 128), 1)
    lanes = jnp.zeros((128, 128), jnp.float32)
    for at, term in enumerate(terms):
        lanes = jnp.where(lane == at, term, lanes)
    return lanes.astype(jnp.bfloat16)


def chunks_of(segments):
    chunks = [[]]
    room = 256
    for k_ref, v_ref, start, count, lanes in segments:
        while count:
            take = min(count, room, 128)
            chunks[-1].append((k_ref, v_ref, start, take, lanes))
            start, count, room = start + take, count - take, room - take
            if not room:
                chunks.append([])
                room = 256
    return [chunk for chunk in chunks if chunk]


def attend(query, segments, scale, before):
    rows = query.shape[0]
    lane = lax.broadcasted_iota(jnp.int32, query.shape, 1)
    query = jnp.concatenate([query, jnp.where(lane < 3, 1.0, 0.0).astype(query.dtype)], axis=1)
    chunks = chunks_of(segments)
    scores = []
    peak = None
    for chunk in chunks:
        keys = jnp.concatenate(
            [
                jnp.concatenate([k_ref[start : start + count, :], lanes[0:count]], axis=1)
                for k_ref, _, start, count, lanes in chunk
            ],
            axis=0,
        )
        score = lax.dot_general(
            query, keys, (((1,), (1,)), ((), ())), preferred_element_type=jnp.float32
        )
        scores.append(score)
        for col in range(0, keys.shape[0], 128):
            top = score[:, col : col + 128]
            peak = top if peak is None else jnp.maximum(peak, top)
    peak = jnp.max(peak, axis=1, keepdims=True) * scale
    if before is not None:
        peak = jnp.maximum(jnp.broadcast_to(peak, before.shape), before)
        lifted = peak[:, 0:1]
    else:
        lifted = peak
    out = None
    for chunk, score in zip(chunks, scores):
        weight = jnp.exp2(score * scale - lifted).astype(jnp.bfloat16)
        values = jnp.concatenate(
            [v_ref[start : start + count, :] for _, v_ref, start, count, _ in chunk], axis=0
        )
        table = jnp.concatenate([values, jnp.ones((values.shape[0], 128), jnp.bfloat16)], axis=1)
        part = jnp.dot(weight, table, preferred_element_type=jnp.float32)
        out = part if out is None else out + part
    return peak, out[:, 0:128], out[:, 128:256]


def base_two_scale(head_size):
    return math.log2(math.e) / math.sqrt(head_size)


def near_kernel(count, dev_ref, q_ref, k_ref, v_ref, l1k, l1v, mk, mv, acc_ref, peak_ref, total_ref):
    scale = base_two_scale(q_ref.shape[1])
    zero = offset_lanes(0, None, scale)
    one = offset_lanes(1, None, scale)
    two = offset_lanes(2, None, scale)
    own = ((256, 256), None, (0, 128), (0, 256))

    def run(odd):
        if odd:
            mate = (
                [(mk, mv, 0, 256, zero), (mk, mv, L1_AT, 128, one), (mk, mv, L2_AT, 128, two)],
                [(mk, mv, L1_AT, 256, one), (mk, mv, L2_AT, 128, two)],
                [(mk, mv, L2_AT, 256, two)],
                [(mk, mv, L2_AT, 256, two)],
            )
        else:
            mate = (
                [(mk, mv, L2_AT, 256, two)],
                [(mk, mv, L1_AT, 128, one), (mk, mv, L2_AT, 256, two)],
                [(mk, mv, L1_AT, 256, one)],
                [(mk, mv, 0, 256, zero), (mk, mv, L1_AT + 256, 128, one)],
            )
        for block in range(BLOCKS):
            low, high = max(block - 1, 0), min(block + 2, BLOCKS)
            segments = [(k_ref, v_ref, low * LEAF, (high - low) * LEAF, zero)]
            if own[block]:
                segments.append((l1k, l1v, own[block][0], own[block][1], one))
            here = slice(block * LEAF, (block + 1) * LEAF)
            peak, acc, total = attend(q_ref[here, :], segments + mate[block], scale, None)
            acc_ref[here, :] = acc
            peak_ref[here, :] = jnp.broadcast_to(peak, acc.shape)
            total_ref[here, :] = total

    @pl.when(dev_ref[0] % 2 == 1)
    def _():
        run(True)

    @pl.when(dev_ref[0] % 2 == 0)
    def _():
        run(False)


def far_kernel(flow_spans, count, dev_ref, q_ref, *refs):
    (xk, xv, i2k, i2v, ownk, ownv, acc_ref, peak_ref, total_ref, out_ref) = refs
    scale = base_two_scale(q_ref.shape[1])
    me = dev_ref[0]
    chip = me // 2
    chips = count // 2

    def lanes(level, valid):
        return offset_lanes(level, valid, scale)

    fours = []
    for shifts in flow_spans:
        valid = False
        for shift in shifts:
            source = chip - shift // 2
            here = (source >= 0) & (source < chips)
            if shift == -4:
                here = here & (chip % 2 == 0)
            if shift == 6:
                here = here & (chip % 2 == 1)
            valid = here | valid
        fours.append(lanes(4, valid))

    def run(odd):
        near = (me < count - 1) if odd else (me >= 1)
        a_ok = (me - 2 >= 0) if odd else (me + 2 < count)
        b_ok = (me + 3 < count) if odd else (me - 2 >= 0)
        c_ok = (me - 3 >= 0) if odd else (me + 3 < count)
        coarse = [
            (i2k, i2v, 128, 128, lanes(3, a_ok)),
            (i2k, i2v, 256, 128, lanes(3, b_ok)),
            (ownk, ownv, 0, 128, lanes(3, c_ok)),
        ]
        for slot, four in enumerate(fours):
            coarse.append((i2k, i2v, 384 + 64 * slot, 64, four))
            coarse.append((ownk, ownv, 128 + 64 * slot, 64, four))
        zero, one, two = (lanes(level, near) for level in range(3))
        skip = (i2k, i2v, 0, 128, lanes(2, me + 2 < count))
        if odd:
            rim = (
                [(xk, xv, L2_AT, 256, two)],
                [(xk, xv, L1_AT, 128, one), (xk, xv, L2_AT, 256, two)],
                [(xk, xv, L1_AT, 256, one), skip],
                [(xk, xv, 0, 256, zero), (xk, xv, L1_AT + 256, 128, one), skip],
            )
        else:
            rim = (
                [(xk, xv, 0, 256, zero), (xk, xv, L1_AT, 128, one), (xk, xv, L2_AT, 128, two)],
                [(xk, xv, L1_AT, 256, one), (xk, xv, L2_AT, 128, two)],
                [(xk, xv, L2_AT, 256, two), skip],
                [(xk, xv, L2_AT, 256, two), skip],
            )
        for block in range(BLOCKS):
            here = slice(block * LEAF, (block + 1) * LEAF)
            before = peak_ref[here, :]
            peak, acc, total = attend(q_ref[here, :], rim[block] + coarse, scale, before)
            factor = jnp.exp2(before - peak)
            acc = acc_ref[here, :] * factor + acc
            total = total_ref[here, :] * factor + total
            out_ref[here, :] = (acc / total).astype(out_ref.dtype)

    @pl.when(me % 2 == 1)
    def _():
        run(True)

    @pl.when(me % 2 == 0)
    def _():
        run(False)


def flow_pairs(shifts, count):
    pairs = []
    for shift in shifts:
        for source in range(count):
            target = source + shift
            if 0 <= target < count and not (shift == 6 and target // 2 % 2 == 0):
                pairs.append((source, target))
    return pairs


def far_flows(count):
    spans = []
    for low, high in ((-4, 4), (-6, 6)):
        pairs = flow_pairs((low, high), count)
        unique = len({s for s, _ in pairs}) == len(pairs) == len({t for _, t in pairs})
        spans.extend([(low, high)] if unique else [(low,), (high,)])
    return tuple(spans)


def on_device(query_rows, key_rows, value_rows):
    token_rows, width = query_rows.shape
    head_size = width // HEADS
    count = lax.axis_size("ctx")
    me = lax.axis_index("ctx").astype(jnp.int32).reshape(1)
    dtype = key_rows.dtype

    def shape(rows, columns=2 * width, kind=dtype):
        return jax.ShapeDtypeStruct((rows, columns), kind)

    smem = pl.BlockSpec(memory_space=pltpu.SMEM)
    vmem = pl.BlockSpec(memory_space=pltpu.VMEM)
    params = pltpu.CompilerParams(vmem_limit_bytes=63 << 20)

    x1s, i1s, x2s, ys, l1 = pl.pallas_call(
        pool_kernel,
        name="pool",
        out_shape=[
            shape(RIM_ROWS), shape(TABLE_ROWS), shape(FAR_ROWS), shape(192), shape(token_rows // 2)
        ],
        in_specs=[smem, vmem, vmem],
        out_specs=[vmem] * 5,
        compiler_params=params,
    )(me, key_rows, value_rows)

    near = range(1, count - 1, 2)
    x1r = lax.ppermute(
        x1s, "ctx", [(i, i + 1) for i in near] + [(i + 1, i) for i in near]
    )
    x2r = lax.ppermute(
        x2s,
        "ctx",
        [(i, i + 3) for i in range(0, count - 3, 2)] + [(i, i - 3) for i in range(3, count, 2)],
    )
    flow_spans = far_flows(count)
    yrs = [lax.ppermute(ys, "ctx", flow_pairs(shifts, count)) for shifts in flow_spans]
    mates = [(i, i ^ 1) for i in range(count)]
    i1r = lax.ppermute(i1s, "ctx", mates)

    def head(rows, base=0):
        return pl.BlockSpec((rows, head_size), lambda h, *_: (0, base + h))

    def cost(keys, rows):
        pairs = token_rows * keys * HEADS
        return pl.CostEstimate(
            flops=4 * pairs * head_size,
            transcendentals=pairs,
            bytes_accessed=rows * 4 * width,
        )

    acc, peak, total = pl.pallas_call(
        functools.partial(near_kernel, count),
        name="near",
        grid=(HEADS,),
        out_shape=[shape(token_rows, width, jnp.float32)] * 3,
        in_specs=[smem]
        + [head(token_rows)] * 3
        + [head(token_rows // 2), head(token_rows // 2, HEADS)]
        + [head(TABLE_ROWS), head(TABLE_ROWS, HEADS)],
        out_specs=[head(token_rows)] * 3,
        compiler_params=params,
        cost_estimate=cost(1152, 6000),
    )(me, query_rows, key_rows, value_rows, l1, l1, i1r, i1r)

    x1r, x2r, yrs, acc, peak, total = lax.optimization_barrier((x1r, x2r, yrs, acc, peak, total))
    share_rows, own_rows = 384 + 64 * len(yrs), 128 + 64 * len(yrs)
    xt, i2s, own = pl.pallas_call(
        share_kernel,
        name="share",
        out_shape=[shape(TABLE_ROWS), shape(share_rows), shape(own_rows)],
        in_specs=[smem] + [vmem] * (2 + len(yrs)),
        out_specs=[vmem] * 3,
        compiler_params=params,
    )(me, x1r, x2r, *yrs)
    i2r = lax.ppermute(i2s, "ctx", mates)

    tables = []
    specs = []
    for table in (xt, i2r, own):
        tables += [table, table]
        specs += [head(table.shape[0]), head(table.shape[0], HEADS)]
    return pl.pallas_call(
        functools.partial(far_kernel, flow_spans, count),
        name="far",
        grid=(HEADS,),
        out_shape=shape(token_rows, width),
        in_specs=[smem, head(token_rows)] + specs + [head(token_rows)] * 3,
        out_specs=head(token_rows),
        compiler_params=params,
        cost_estimate=cost(1152, 6000),
    )(me, query_rows, *tables, acc, peak, total)


def solution(mesh):
    spec = P(("dp", "ctx"), None)
    return jax.shard_map(
        on_device, mesh=mesh, in_specs=(spec, spec, spec), out_specs=spec, check_vma=False
    )
```

```python
import functools
import math

import jax
import jax.numpy as jnp
import ml_dtypes
import numpy as np
from jax import lax
from jax.experimental import pallas as pl
from jax.experimental.pallas import tpu as pltpu
from jax.sharding import PartitionSpec as P

HEADS = 4
LEAF = 256
LEVELS = 5
HALF = LEAF // 2
BLOCKS = 4
EDGE_ROWS = 256
RIM_ROWS = 320
TABLE_ROWS = 896
L1_AT = 256
L2_AT = 640
FAR_ROWS = 192
HIDDEN = -1e30


def pooled(x, wide_ref):
    rows, width = x.shape
    parts = []
    for at in range(width // 128):
        wide_ref[at, 0:rows, :] = x[:, at * 128 : (at + 1) * 128].astype(jnp.float32)
        even = wide_ref[at, pl.ds(0, rows // 2, stride=2), :]
        odd = wide_ref[at, pl.ds(1, rows // 2, stride=2), :]
        parts.append(((even + odd) * 0.5).astype(x.dtype))
    return jnp.concatenate(parts, axis=1) if len(parts) > 1 else parts[0]


def pool_kernel(
    dev_ref, k_ref, v_ref, edge_ref, x1_ref, i1_ref, x2_ref, y_ref, l4_ref, l1_ref, wide_ref
):
    odd = dev_ref[0] % 2 == 1
    steps = pl.num_programs(0) // 2
    at = pl.program_id(0)

    def write(l0):
        l1 = pooled(l0[...], wide_ref)
        l2 = pooled(l1, wide_ref)
        l3 = pooled(l2, wide_ref)
        l4 = pooled(l3, wide_ref)
        l1_ref[...] = l1
        y_ref[0:128, :] = l3
        y_ref[128:192, :] = l4
        l4_ref[...] = l4
        i1_ref[L2_AT:TABLE_ROWS, :] = l2

        @pl.when(odd)
        def _():
            edge_ref[...] = l0[768:1024, :]
            x1_ref[0:128, :] = l1[256:384]
            x1_ref[128:256, :] = l2[0:128]
            x1_ref[256:320, :] = l2[0:64]
            i1_ref[0:256, :] = l0[0:256, :]
            i1_ref[L1_AT:L2_AT, :] = l1[0:384]
            x2_ref[0:128, :] = l2[0:128]
            x2_ref[128:192, :] = l3[64:128]

        @pl.when(jnp.logical_not(odd))
        def _():
            edge_ref[...] = l0[0:256, :]
            x1_ref[0:256, :] = l1[128:384]
            x1_ref[256:320, :] = l2[192:256]
            i1_ref[0:256, :] = l0[768:1024, :]
            i1_ref[L1_AT : L1_AT + 256, :] = l1[256:512]
            i1_ref[L1_AT + 256 : L2_AT, :] = l1[0:128]
            x2_ref[0:128, :] = l3
            x2_ref[128:192, :] = l3[64:128]

    @pl.when(at < steps)
    def _():
        write(k_ref)

    @pl.when(at >= steps)
    def _():
        write(v_ref)


def rim_kernel(relayed, dev_ref, edge_ref, via_ref, x1_ref, xt_ref, i2_ref, wide_ref):
    me = dev_ref[0]
    odd = me % 2 == 1
    if relayed:
        twice = functools.reduce(jnp.logical_or, [me == target for target in relayed])

        @pl.when(twice)
        def _():
            xt_ref[0:256, :] = via_ref[...]

        @pl.when(jnp.logical_not(twice))
        def _():
            xt_ref[0:256, :] = edge_ref[...]
    else:
        xt_ref[0:256, :] = edge_ref[...]

    @pl.when(odd)
    def _():
        l1 = jnp.concatenate([pooled(xt_ref[0:256, :], wide_ref), x1_ref[0:256, :]], axis=0)
        l2 = jnp.concatenate([pooled(l1, wide_ref), x1_ref[256:320, :]], axis=0)
        xt_ref[L1_AT:L2_AT, :] = l1
        xt_ref[L2_AT:TABLE_ROWS, :] = l2
        i2_ref[0:128, :] = l2[0:128]
        i2_ref[128:256, :] = pooled(l2, wide_ref)

    @pl.when(jnp.logical_not(odd))
    def _():
        l1 = jnp.concatenate([x1_ref[0:128, :], pooled(xt_ref[0:256, :], wide_ref)], axis=0)
        l2 = jnp.concatenate([x1_ref[128:256, :], pooled(l1, wide_ref)], axis=0)
        xt_ref[L1_AT : L1_AT + 256, :] = l1
        xt_ref[L1_AT + 256 : L2_AT, :] = l1[0:128]
        xt_ref[L2_AT:TABLE_ROWS, :] = l2
        l3 = pooled(l2, wide_ref)
        i2_ref[0:128, :] = l3
        i2_ref[128:256, :] = l3


def offset_lanes(level, valid, scale):
    terms = []
    rest = level / scale
    for _ in range(3):
        term = float(np.float32(rest).astype(ml_dtypes.bfloat16))
        terms.append(term)
        rest -= term
    if valid is not None:
        terms = [jnp.where(valid, t, h) for t, h in zip(terms, (HIDDEN, 0.0, 0.0))]
    lane = lax.broadcasted_iota(jnp.int32, (128, 128), 1)
    lanes = jnp.zeros((128, 128), jnp.float32)
    for at, term in enumerate(terms):
        lanes = jnp.where(lane == at, term, lanes)
    return lanes.astype(jnp.bfloat16)


def chunks_of(segments):
    chunks = [[]]
    room = 256
    for k_ref, v_ref, start, count, lanes in segments:
        while count:
            take = min(count, room, 128)
            chunks[-1].append((k_ref, v_ref, start, take, lanes))
            start, count, room = start + take, count - take, room - take
            if not room:
                chunks.append([])
                room = 256
    return [chunk for chunk in chunks if chunk]


def attend(query, segments, scale, before):
    rows = query.shape[0]
    lane = lax.broadcasted_iota(jnp.int32, query.shape, 1)
    query = jnp.concatenate([query, jnp.where(lane < 3, 1.0, 0.0).astype(query.dtype)], axis=1)
    chunks = chunks_of(segments)
    scores = []
    peak = None
    for chunk in chunks:
        keys = jnp.concatenate(
            [
                jnp.concatenate([k_ref[start : start + count, :], lanes[0:count]], axis=1)
                for k_ref, _, start, count, lanes in chunk
            ],
            axis=0,
        )
        score = lax.dot_general(
            query, keys, (((1,), (1,)), ((), ())), preferred_element_type=jnp.float32
        )
        scores.append(score)
        for col in range(0, keys.shape[0], 128):
            top = score[:, col : col + 128]
            peak = top if peak is None else jnp.maximum(peak, top)
    peak = jnp.max(peak, axis=1, keepdims=True) * scale
    if before is not None:
        peak = jnp.maximum(peak, before)
    out = None
    for chunk, score in zip(chunks, scores):
        weight = jnp.exp2(score * scale - peak).astype(jnp.bfloat16)
        values = jnp.concatenate(
            [v_ref[start : start + count, :] for _, v_ref, start, count, _ in chunk], axis=0
        )
        table = jnp.concatenate([values, jnp.ones((values.shape[0], 128), jnp.bfloat16)], axis=1)
        part = jnp.dot(weight, table, preferred_element_type=jnp.float32)
        out = part if out is None else out + part
    return peak, out[:, 0:128], out[:, 128:256]


def base_two_scale(head_size):
    return math.log2(math.e) / math.sqrt(head_size)


def near_kernel(dev_ref, q_ref, k_ref, v_ref, l1k, l1v, mk, mv, *sums):
    scale = base_two_scale(q_ref.shape[1])
    zero = offset_lanes(0, None, scale)
    one = offset_lanes(1, None, scale)
    two = offset_lanes(2, None, scale)
    own = ((256, 256), None, (0, 128), (0, 256))

    def run(odd):
        if odd:
            mate = (
                [(mk, mv, 0, 256, zero), (mk, mv, L1_AT, 128, one), (mk, mv, L2_AT, 128, two)],
                [(mk, mv, L1_AT, 256, one), (mk, mv, L2_AT, 128, two)],
                [(mk, mv, L2_AT, 256, two)],
                [(mk, mv, L2_AT, 256, two)],
            )
        else:
            mate = (
                [(mk, mv, L2_AT, 256, two)],
                [(mk, mv, L1_AT, 128, one), (mk, mv, L2_AT, 256, two)],
                [(mk, mv, L1_AT, 256, one)],
                [(mk, mv, 0, 256, zero), (mk, mv, L1_AT + 256, 128, one)],
            )
        for block in range(BLOCKS):
            low, high = max(block - 1, 0), min(block + 2, BLOCKS)
            segments = [(k_ref, v_ref, low * LEAF, (high - low) * LEAF, zero)]
            if own[block]:
                segments.append((l1k, l1v, own[block][0], own[block][1], one))
            here = slice(block * LEAF, (block + 1) * LEAF)
            peak, acc, total = attend(q_ref[here, :], segments + mate[block], scale, None)
            write_sums(sums, here, peak, acc, total)

    @pl.when(dev_ref[0] % 2 == 1)
    def _():
        run(True)

    @pl.when(dev_ref[0] % 2 == 0)
    def _():
        run(False)


def read_mass(mass_ref, here):
    packed = mass_ref[here, :]
    lane = lax.broadcasted_iota(jnp.int32, packed.shape, 1)
    own = jnp.where(lane == pl.program_id(0), packed, 0.0)
    return jnp.sum(own, axis=1, keepdims=True)


def write_sums(sums, here, peak, acc, total):
    mean_ref, mass_ref = sums
    mean_ref[here, :] = acc / total
    lane = lax.broadcasted_iota(jnp.int32, acc.shape, 1)
    mass = peak + jnp.log2(total)
    kept = jnp.where(pl.program_id(0) == 0, 0.0, mass_ref[here, :])
    mass_ref[here, :] = jnp.where(lane == pl.program_id(0), mass, kept)


def attend_after(query, segments, scale, stats, here):
    mean_ref, mass_ref = stats
    mass = read_mass(mass_ref, here)
    peak, acc, total = attend(query, segments, scale, mass)
    factor = jnp.exp2(mass - peak)
    return peak, mean_ref[here, :] * factor + acc, total + factor


def far_kernel(flow_spans, count, dev_ref, q_ref, *refs):
    xk, xv, i2k, i2v, x2k, x2v, x2mk, x2mv = refs[0:8]
    stats, out_ref, wide_ref = refs[-4:-2], refs[-2], refs[-1]
    flow_refs = [refs[8 + 4 * at : 12 + 4 * at] for at in range(len(flow_spans))]
    scale = base_two_scale(q_ref.shape[1])
    me = dev_ref[0]
    chip = me // 2
    chips = count // 2

    def lanes(level, valid):
        return offset_lanes(level, valid, scale)

    quads = []
    for shifts, (yk, yv, ymk, ymv) in zip(flow_spans, flow_refs):
        valid = False
        for shift in shifts:
            source = chip - shift // 2
            here = (source >= 0) & (source < chips)
            if shift == -4:
                here = here & (chip % 2 == 0)
            if shift == 6:
                here = here & (chip % 2 == 1)
            valid = here | valid
        four = lanes(4, valid)
        start = yk.shape[0] - 64
        quads += [(yk, yv, start, 64, four), (ymk, ymv, start, 64, four)]

    def run(odd):
        near = (me < count - 1) if odd else (me >= 1)
        zero, one, two = (lanes(level, near) for level in range(3))
        beyond = lanes(2, me + 2 < count)
        if odd:
            ymk, ymv = flow_refs[0][2:4]
            coarse = [
                (ymk, ymv, 0, 128, lanes(3, me + 3 < count)),
                (x2k, x2v, 0, 128, lanes(3, me - 3 >= 0)),
                (i2k, i2v, 0, 128, lanes(3, me - 2 >= 0)),
            ]
            skip = (x2mk, x2mv, 0, 128, beyond)
            rim = (
                [(xk, xv, L2_AT, 256, two)],
                [(xk, xv, L2_AT, 256, two), (xk, xv, L1_AT, 128, one)],
                [(xk, xv, L1_AT, 256, one), skip],
                [(xk, xv, 0, 256, zero), (xk, xv, L1_AT + 256, 128, one), skip],
            )
        else:
            third = [
                jnp.concatenate([pooled(table[0:128, :], wide_ref), table[128:192, :]], axis=0)
                for table in (x2k, x2v)
            ]
            coarse = [
                (x2mk, x2mv, 0, 128, lanes(3, me - 2 >= 0)),
                (third[0], third[1], 0, 128, lanes(3, me + 3 < count)),
                (i2k, i2v, 128, 128, lanes(3, me + 2 < count)),
            ]
            skip = (i2k, i2v, 0, 128, beyond)
            rim = (
                [(xk, xv, 0, 256, zero), (xk, xv, L1_AT, 128, one), (xk, xv, L2_AT, 128, two)],
                [(xk, xv, L1_AT, 256, one), (xk, xv, L2_AT, 128, two)],
                [(xk, xv, L2_AT, 256, two), skip],
                [(xk, xv, L2_AT, 256, two), skip],
            )
        for block in range(BLOCKS):
            here = slice(block * LEAF, (block + 1) * LEAF)
            segments = quads + coarse[0:2] + rim[block] + coarse[2:3]
            _, acc, total = attend_after(q_ref[here, :], segments, scale, stats, here)
            out_ref[here, :] = (acc / total).astype(out_ref.dtype)

    @pl.when(me % 2 == 1)
    def _():
        run(True)

    @pl.when(me % 2 == 0)
    def _():
        run(False)


def relays(count):
    return {(3, 4): 7, (4, 3): 0} if count == 8 else {}


def flow_pairs(shifts, count):
    pairs = []
    for shift in shifts:
        for source in range(count):
            target = source + shift
            if 0 <= target < count and not (shift == 6 and target // 2 % 2 == 0):
                pairs.append((source, target))
    return pairs


def far_flows(count):
    spans = []
    for low, high in ((-4, 4), (-6, 6)):
        pairs = flow_pairs((low, high), count)
        unique = len({s for s, _ in pairs}) == len(pairs) == len({t for _, t in pairs})
        spans.extend([(low, high)] if unique else [(low,), (high,)])
    return tuple(spans)


def on_device(query_rows, key_rows, value_rows):
    token_rows, width = query_rows.shape
    head_size = width // HEADS
    count = lax.axis_size("ctx")
    me = lax.axis_index("ctx").astype(jnp.int32).reshape(1)
    dtype = key_rows.dtype

    def shape(rows, columns=2 * width, kind=dtype):
        return jax.ShapeDtypeStruct((rows, columns), kind)

    smem = pl.BlockSpec(memory_space=pltpu.SMEM)
    params = pltpu.CompilerParams(vmem_limit_bytes=64 << 20)

    near = range(1, count - 1, 2)
    across = [(i, i + 1) for i in near] + [(i + 1, i) for i in near]
    detours = relays(count)
    cut = width

    def column(rows):
        return pl.BlockSpec((rows, cut), lambda j: (0, j))

    pooled_rows = (EDGE_ROWS, RIM_ROWS, TABLE_ROWS, FAR_ROWS, 192, 64, token_rows // 2)
    edge, x1s, i1s, x2s, ys, l4, l1 = pl.pallas_call(
        pool_kernel,
        name="pool",
        grid=(2,),
        out_shape=[shape(rows) for rows in pooled_rows],
        in_specs=[
            smem,
            pl.BlockSpec((token_rows, cut), lambda j: (0, 0)),
            pl.BlockSpec((token_rows, cut), lambda j: (0, 0)),
        ],
        out_specs=[column(rows) for rows in pooled_rows],
        scratch_shapes=[pltpu.VMEM((cut // 128, token_rows, 128), jnp.float32)],
        compiler_params=params,
        cost_estimate=pl.CostEstimate(flops=0, transcendentals=0, bytes_accessed=24 << 20),
    )(me, key_rows, value_rows)

    edge_r = lax.ppermute(edge, "ctx", [(s, detours.get((s, t), t)) for s, t in across])
    x2r = lax.ppermute(
        x2s,
        "ctx",
        [(i, i + 3) for i in range(0, count - 3, 2)] + [(i, i - 3) for i in range(3, count, 2)],
    )
    flow_spans = far_flows(count)
    yrs = [
        lax.ppermute(ys if abs(shifts[0]) == 4 else l4, "ctx", flow_pairs(shifts, count))
        for shifts in flow_spans
    ]
    x1r = lax.ppermute(x1s, "ctx", across)
    mates = [(i, i ^ 1) for i in range(count)]
    i1r = lax.ppermute(i1s, "ctx", mates)
    edge_r, i1r = lax.optimization_barrier((edge_r, i1r))
    via_r = edge_r
    if detours:
        via_r = lax.ppermute(edge_r, "ctx", [(via, t) for (_, t), via in detours.items()])

    def head(rows, base=0):
        return pl.BlockSpec((rows, head_size), lambda h, *_: (0, base + h))

    def attention(kernel, name, keys, tables, stats, last=False):
        arrays, specs = [], []
        for table in tables:
            if isinstance(table, tuple):
                arrays += table
                specs += [head(table[0].shape[0])] * 2
            else:
                arrays += [table, table]
                specs += [head(table.shape[0]), head(table.shape[0], HEADS)]
        pairs = token_rows * keys * HEADS
        sums = [shape(token_rows, width, jnp.float32), shape(token_rows, 128, jnp.float32)]
        sum_specs = [head(token_rows), pl.BlockSpec((token_rows, 128), lambda h: (0, 0))]
        return pl.pallas_call(
            kernel,
            name=name,
            grid=(HEADS,),
            out_shape=shape(token_rows, width) if last else sums,
            in_specs=[smem, head(token_rows)] + specs + (sum_specs if stats else []),
            out_specs=head(token_rows) if last else sum_specs,
            scratch_shapes=[pltpu.VMEM((head_size // 128, 128, 128), jnp.float32)] if last else [],
            compiler_params=params,
            cost_estimate=pl.CostEstimate(
                flops=4 * pairs * head_size, transcendentals=pairs, bytes_accessed=12 << 20
            ),
        )(me, query_rows, *arrays, *stats)

    stats = attention(
        near_kernel,
        "near",
        1152,
        [(key_rows, value_rows), l1, i1r],
        (),
    )
    x2r, yrs, stats = lax.optimization_barrier((x2r, yrs, stats))
    tables = [x2r, lax.ppermute(x2r, "ctx", mates)]
    for yr in yrs:
        tables += [yr, lax.ppermute(yr, "ctx", mates)]
    edge_r, via_r, x1r, stats = lax.optimization_barrier((edge_r, via_r, x1r, stats))
    xt, i2s = pl.pallas_call(
        functools.partial(rim_kernel, [t for _, t in detours]),
        name="rim",
        grid=(2,),
        out_shape=[shape(TABLE_ROWS), shape(256)],
        in_specs=[smem, column(EDGE_ROWS), column(EDGE_ROWS), column(RIM_ROWS)],
        out_specs=[column(TABLE_ROWS), column(256)],
        scratch_shapes=[pltpu.VMEM((cut // 128, 384, 128), jnp.float32)],
        compiler_params=params,
    )(me, edge_r, via_r, x1r)
    i2r = lax.ppermute(i2s, "ctx", mates)
    kernel = functools.partial(far_kernel, flow_spans, count)
    return attention(kernel, "far", 1088, [xt, i2r] + tables, stats, True)


def solution(mesh):
    spec = P(("dp", "ctx"), None)
    return jax.shard_map(
        on_device, mesh=mesh, in_specs=(spec, spec, spec), out_specs=spec, check_vma=False
    )
```

```python
import functools
import math

import jax
import jax.numpy as jnp
import ml_dtypes
import numpy as np
from jax import lax
from jax.experimental import pallas as pl
from jax.experimental.pallas import tpu as pltpu
from jax.sharding import PartitionSpec as P

HEADS = 4
LEAF = 256
LEVELS = 5
HALF = LEAF // 2
BLOCKS = 4
EDGE_ROWS = 256
RIM_ROWS = 320
TABLE_ROWS = 896
L1_AT = 256
L2_AT = 640
FAR_ROWS = 192
HIDDEN = -1e30
SAFE_TOTAL = 2.0**100


def pooled(x, wide_ref):
    rows, width = x.shape
    parts = []
    for at in range(width // 128):
        wide_ref[at, 0:rows, :] = x[:, at * 128 : (at + 1) * 128].astype(jnp.float32)
        even = wide_ref[at, pl.ds(0, rows // 2, stride=2), :]
        odd = wide_ref[at, pl.ds(1, rows // 2, stride=2), :]
        parts.append(((even + odd) * 0.5).astype(x.dtype))
    return jnp.concatenate(parts, axis=1) if len(parts) > 1 else parts[0]


def pool_kernel(
    dev_ref, k_ref, v_ref, edge_ref, x1_ref, i1_ref, x2_ref, y_ref, l4_ref, l1_ref, wide_ref
):
    odd = dev_ref[0] % 2 == 1
    steps = pl.num_programs(0) // 2
    at = pl.program_id(0)

    def write(l0):
        l1 = pooled(l0[...], wide_ref)
        l2 = pooled(l1, wide_ref)
        l3 = pooled(l2, wide_ref)
        l4 = pooled(l3, wide_ref)
        l1_ref[...] = l1
        y_ref[0:128, :] = l3
        y_ref[128:192, :] = l4
        l4_ref[...] = l4
        i1_ref[L2_AT:TABLE_ROWS, :] = l2

        @pl.when(odd)
        def _():
            edge_ref[...] = l0[768:1024, :]
            x1_ref[0:128, :] = l1[256:384]
            x1_ref[128:256, :] = l2[0:128]
            x1_ref[256:320, :] = l2[0:64]
            i1_ref[0:256, :] = l0[0:256, :]
            i1_ref[L1_AT:L2_AT, :] = l1[0:384]
            x2_ref[0:128, :] = l2[0:128]
            x2_ref[128:192, :] = l3[64:128]

        @pl.when(jnp.logical_not(odd))
        def _():
            edge_ref[...] = l0[0:256, :]
            x1_ref[0:256, :] = l1[128:384]
            x1_ref[256:320, :] = l2[192:256]
            i1_ref[0:256, :] = l0[768:1024, :]
            i1_ref[L1_AT : L1_AT + 256, :] = l1[256:512]
            i1_ref[L1_AT + 256 : L2_AT, :] = l1[0:128]
            x2_ref[0:128, :] = l3
            x2_ref[128:192, :] = l3[64:128]

    @pl.when(at < steps)
    def _():
        write(k_ref)

    @pl.when(at >= steps)
    def _():
        write(v_ref)


def rim_kernel(relayed, dev_ref, edge_ref, via_ref, x1_ref, xt_ref, i2_ref, wide_ref):
    me = dev_ref[0]
    odd = me % 2 == 1
    if relayed:
        twice = functools.reduce(jnp.logical_or, [me == target for target in relayed])

        @pl.when(twice)
        def _():
            xt_ref[0:256, :] = via_ref[...]

        @pl.when(jnp.logical_not(twice))
        def _():
            xt_ref[0:256, :] = edge_ref[...]
    else:
        xt_ref[0:256, :] = edge_ref[...]

    @pl.when(odd)
    def _():
        l1 = jnp.concatenate([pooled(xt_ref[0:256, :], wide_ref), x1_ref[0:256, :]], axis=0)
        l2 = jnp.concatenate([pooled(l1, wide_ref), x1_ref[256:320, :]], axis=0)
        xt_ref[L1_AT:L2_AT, :] = l1
        xt_ref[L2_AT:TABLE_ROWS, :] = l2
        i2_ref[0:128, :] = l2[0:128]
        i2_ref[128:256, :] = pooled(l2, wide_ref)

    @pl.when(jnp.logical_not(odd))
    def _():
        l1 = jnp.concatenate([x1_ref[0:128, :], pooled(xt_ref[0:256, :], wide_ref)], axis=0)
        l2 = jnp.concatenate([x1_ref[128:256, :], pooled(l1, wide_ref)], axis=0)
        xt_ref[L1_AT : L1_AT + 256, :] = l1
        xt_ref[L1_AT + 256 : L2_AT, :] = l1[0:128]
        xt_ref[L2_AT:TABLE_ROWS, :] = l2
        l3 = pooled(l2, wide_ref)
        i2_ref[0:128, :] = l3
        i2_ref[128:256, :] = l3


def offset_lanes(level, valid, scale):
    terms = []
    rest = level / scale
    for _ in range(3):
        term = float(np.float32(rest).astype(ml_dtypes.bfloat16))
        terms.append(term)
        rest -= term
    if valid is not None:
        terms = [jnp.where(valid, t, h) for t, h in zip(terms, (HIDDEN, 0.0, 0.0))]
    lane = lax.broadcasted_iota(jnp.int32, (128, 128), 1)
    lanes = jnp.zeros((128, 128), jnp.float32)
    for at, term in enumerate(terms):
        lanes = jnp.where(lane == at, term, lanes)
    return lanes.astype(jnp.bfloat16)


def chunks_of(segments):
    chunks = [[]]
    room = 256
    for k_ref, v_ref, start, count, lanes in segments:
        while count:
            take = min(count, room, 128)
            chunks[-1].append((k_ref, v_ref, start, take, lanes))
            start, count, room = start + take, count - take, room - take
            if not room:
                chunks.append([])
                room = 256
    return [chunk for chunk in chunks if chunk]


def attend(query, segments, scale, before, exact):
    rows = query.shape[0]
    lane = lax.broadcasted_iota(jnp.int32, query.shape, 1)
    query = jnp.concatenate([query, jnp.where(lane < 3, 1.0, 0.0).astype(query.dtype)], axis=1)
    chunks = chunks_of(segments)
    scores = []
    peak = None
    for chunk in chunks:
        keys = jnp.concatenate(
            [
                jnp.concatenate([k_ref[start : start + count, :], lanes[0:count]], axis=1)
                for k_ref, _, start, count, lanes in chunk
            ],
            axis=0,
        )
        score = lax.dot_general(
            query, keys, (((1,), (1,)), ((), ())), preferred_element_type=jnp.float32
        )
        scores.append(score)
        if not exact and (peak is not None or before is not None):
            continue
        for col in range(0, keys.shape[0], 128):
            top = score[:, col : col + 128]
            peak = top if peak is None else jnp.maximum(peak, top)
    if peak is None:
        peak = before
    else:
        peak = jnp.max(peak, axis=1, keepdims=True) * scale
        if before is not None:
            peak = jnp.maximum(peak, before)
    out = None
    for chunk, score in zip(chunks, scores):
        weight = jnp.exp2(score * scale - peak).astype(jnp.bfloat16)
        values = jnp.concatenate(
            [v_ref[start : start + count, :] for _, v_ref, start, count, _ in chunk], axis=0
        )
        table = jnp.concatenate([values, jnp.ones((values.shape[0], 128), jnp.bfloat16)], axis=1)
        part = jnp.dot(weight, table, preferred_element_type=jnp.float32)
        out = part if out is None else out + part
    return peak, out[:, 0:128], out[:, 128:256]


def base_two_scale(head_size):
    return math.log2(math.e) / math.sqrt(head_size)


def near_kernel(dev_ref, q_ref, k_ref, v_ref, l1k, l1v, mk, mv, *sums):
    scale = base_two_scale(q_ref.shape[1])
    zero = offset_lanes(0, None, scale)
    one = offset_lanes(1, None, scale)
    two = offset_lanes(2, None, scale)
    own = ((256, 256), None, (0, 128), (0, 256))

    def run(odd):
        if odd:
            mate = (
                [(mk, mv, 0, 256, zero), (mk, mv, L1_AT, 128, one), (mk, mv, L2_AT, 128, two)],
                [(mk, mv, L1_AT, 256, one), (mk, mv, L2_AT, 128, two)],
                [(mk, mv, L2_AT, 256, two)],
                [(mk, mv, L2_AT, 256, two)],
            )
        else:
            mate = (
                [(mk, mv, L2_AT, 256, two)],
                [(mk, mv, L1_AT, 128, one), (mk, mv, L2_AT, 256, two)],
                [(mk, mv, L1_AT, 256, one)],
                [(mk, mv, 0, 256, zero), (mk, mv, L1_AT + 256, 128, one)],
            )
        def one_block(block, exact):
            low, high = max(block - 1, 0), min(block + 2, BLOCKS)
            segments = [(k_ref, v_ref, low * LEAF, (high - low) * LEAF, zero)]
            if own[block]:
                segments.append((l1k, l1v, own[block][0], own[block][1], one))
            here = slice(block * LEAF, (block + 1) * LEAF)
            peak, acc, total = attend(q_ref[here, :], segments + mate[block], scale, None, exact)
            write_sums(sums, here, peak, acc, total)
            return total

        all_blocks(one_block)

    @pl.when(dev_ref[0] % 2 == 1)
    def _():
        run(True)

    @pl.when(dev_ref[0] % 2 == 0)
    def _():
        run(False)


def read_mass(mass_ref, here):
    packed = mass_ref[here, :]
    lane = lax.broadcasted_iota(jnp.int32, packed.shape, 1)
    own = jnp.where(lane == pl.program_id(0), packed, 0.0)
    return jnp.sum(own, axis=1, keepdims=True)


def write_sums(sums, here, peak, acc, total):
    mean_ref, mass_ref = sums
    mean_ref[here, :] = acc / total
    lane = lax.broadcasted_iota(jnp.int32, acc.shape, 1)
    mass = peak + jnp.log2(total)
    kept = jnp.where(pl.program_id(0) == 0, 0.0, mass_ref[here, :])
    mass_ref[here, :] = jnp.where(lane == pl.program_id(0), mass, kept)


def all_blocks(one_block):
    largest = None
    for block in range(BLOCKS):
        total = one_block(block, False)
        largest = total if largest is None else jnp.maximum(largest, total)

    @pl.when(jnp.logical_not(jnp.max(largest) < SAFE_TOTAL))
    def _():
        for block in range(BLOCKS):
            one_block(block, True)


def attend_after(query, segments, scale, stats, here, exact):
    mean_ref, mass_ref = stats
    mass = read_mass(mass_ref, here)
    peak, acc, total = attend(query, segments, scale, mass, exact)
    if not exact:
        return peak, mean_ref[here, :] + acc, total + 1.0
    factor = jnp.exp2(mass - peak)
    return peak, mean_ref[here, :] * factor + acc, total + factor


def far_kernel(flow_spans, count, dev_ref, q_ref, *refs):
    xk, xv, i2k, i2v, x2k, x2v, x2mk, x2mv = refs[0:8]
    stats, out_ref, wide_ref = refs[-4:-2], refs[-2], refs[-1]
    flow_refs = [refs[8 + 4 * at : 12 + 4 * at] for at in range(len(flow_spans))]
    scale = base_two_scale(q_ref.shape[1])
    me = dev_ref[0]
    chip = me // 2
    chips = count // 2

    def lanes(level, valid):
        return offset_lanes(level, valid, scale)

    quads = []
    for shifts, (yk, yv, ymk, ymv) in zip(flow_spans, flow_refs):
        valid = False
        for shift in shifts:
            source = chip - shift // 2
            here = (source >= 0) & (source < chips)
            if shift == -4:
                here = here & (chip % 2 == 0)
            if shift == 6:
                here = here & (chip % 2 == 1)
            valid = here | valid
        four = lanes(4, valid)
        start = yk.shape[0] - 64
        quads += [(yk, yv, start, 64, four), (ymk, ymv, start, 64, four)]

    def run(odd):
        near = (me < count - 1) if odd else (me >= 1)
        zero, one, two = (lanes(level, near) for level in range(3))
        beyond = lanes(2, me + 2 < count)
        if odd:
            ymk, ymv = flow_refs[0][2:4]
            coarse = [
                (ymk, ymv, 0, 128, lanes(3, me + 3 < count)),
                (x2k, x2v, 0, 128, lanes(3, me - 3 >= 0)),
                (i2k, i2v, 0, 128, lanes(3, me - 2 >= 0)),
            ]
            skip = (x2mk, x2mv, 0, 128, beyond)
            rim = (
                [(xk, xv, L2_AT, 256, two)],
                [(xk, xv, L2_AT, 256, two), (xk, xv, L1_AT, 128, one)],
                [(xk, xv, L1_AT, 256, one), skip],
                [(xk, xv, 0, 256, zero), (xk, xv, L1_AT + 256, 128, one), skip],
            )
        else:
            third = [
                jnp.concatenate([pooled(table[0:128, :], wide_ref), table[128:192, :]], axis=0)
                for table in (x2k, x2v)
            ]
            coarse = [
                (x2mk, x2mv, 0, 128, lanes(3, me - 2 >= 0)),
                (third[0], third[1], 0, 128, lanes(3, me + 3 < count)),
                (i2k, i2v, 128, 128, lanes(3, me + 2 < count)),
            ]
            skip = (i2k, i2v, 0, 128, beyond)
            rim = (
                [(xk, xv, 0, 256, zero), (xk, xv, L1_AT, 128, one), (xk, xv, L2_AT, 128, two)],
                [(xk, xv, L1_AT, 256, one), (xk, xv, L2_AT, 128, two)],
                [(xk, xv, L2_AT, 256, two), skip],
                [(xk, xv, L2_AT, 256, two), skip],
            )
        def one_block(block, exact):
            here = slice(block * LEAF, (block + 1) * LEAF)
            segments = quads + coarse[0:2] + rim[block] + coarse[2:3]
            _, acc, total = attend_after(q_ref[here, :], segments, scale, stats, here, exact)
            out_ref[here, :] = (acc / total).astype(out_ref.dtype)
            return total

        all_blocks(one_block)

    @pl.when(me % 2 == 1)
    def _():
        run(True)

    @pl.when(me % 2 == 0)
    def _():
        run(False)


def relays(count):
    return {(3, 4): 7, (4, 3): 0} if count == 8 else {}


def flow_pairs(shifts, count):
    pairs = []
    for shift in shifts:
        for source in range(count):
            target = source + shift
            if 0 <= target < count and not (shift == 6 and target // 2 % 2 == 0):
                pairs.append((source, target))
    return pairs


def far_flows(count):
    spans = []
    for low, high in ((-4, 4), (-6, 6)):
        pairs = flow_pairs((low, high), count)
        unique = len({s for s, _ in pairs}) == len(pairs) == len({t for _, t in pairs})
        spans.extend([(low, high)] if unique else [(low,), (high,)])
    return tuple(spans)


def on_device(query_rows, key_rows, value_rows):
    token_rows, width = query_rows.shape
    head_size = width // HEADS
    count = lax.axis_size("ctx")
    me = lax.axis_index("ctx").astype(jnp.int32).reshape(1)
    dtype = key_rows.dtype

    def shape(rows, columns=2 * width, kind=dtype):
        return jax.ShapeDtypeStruct((rows, columns), kind)

    smem = pl.BlockSpec(memory_space=pltpu.SMEM)
    params = pltpu.CompilerParams(vmem_limit_bytes=64 << 20)

    near = range(1, count - 1, 2)
    across = [(i, i + 1) for i in near] + [(i + 1, i) for i in near]
    detours = relays(count)
    cut = width

    def column(rows):
        return pl.BlockSpec((rows, cut), lambda j: (0, j))

    pooled_rows = (EDGE_ROWS, RIM_ROWS, TABLE_ROWS, FAR_ROWS, 192, 64, token_rows // 2)
    edge, x1s, i1s, x2s, ys, l4, l1 = pl.pallas_call(
        pool_kernel,
        name="pool",
        grid=(2,),
        out_shape=[shape(rows) for rows in pooled_rows],
        in_specs=[
            smem,
            pl.BlockSpec((token_rows, cut), lambda j: (0, 0)),
            pl.BlockSpec((token_rows, cut), lambda j: (0, 0)),
        ],
        out_specs=[column(rows) for rows in pooled_rows],
        scratch_shapes=[pltpu.VMEM((cut // 128, token_rows, 128), jnp.float32)],
        compiler_params=params,
        cost_estimate=pl.CostEstimate(flops=0, transcendentals=0, bytes_accessed=24 << 20),
    )(me, key_rows, value_rows)

    edge_r = lax.ppermute(edge, "ctx", [(s, detours.get((s, t), t)) for s, t in across])
    x2r = lax.ppermute(
        x2s,
        "ctx",
        [(i, i + 3) for i in range(0, count - 3, 2)] + [(i, i - 3) for i in range(3, count, 2)],
    )
    flow_spans = far_flows(count)
    steps = [shifts for shifts in flow_spans if abs(shifts[0]) == 4]
    yrs = [lax.ppermute(ys, "ctx", flow_pairs(shifts, count)) for shifts in steps]
    x1r = lax.ppermute(x1s, "ctx", across)
    mates = [(i, i ^ 1) for i in range(count)]
    i1r = lax.ppermute(i1s, "ctx", mates)

    def head(rows, base=0):
        return pl.BlockSpec((rows, head_size), lambda h, *_: (0, base + h))

    def attention(kernel, name, keys, tables, stats, last=False):
        arrays, specs = [], []
        for table in tables:
            if isinstance(table, tuple):
                arrays += table
                specs += [head(table[0].shape[0])] * 2
            else:
                arrays += [table, table]
                specs += [head(table.shape[0]), head(table.shape[0], HEADS)]
        pairs = token_rows * keys * HEADS
        sums = [shape(token_rows, width, jnp.float32), shape(token_rows, 128, jnp.float32)]
        sum_specs = [head(token_rows), pl.BlockSpec((token_rows, 128), lambda h: (0, 0))]
        return pl.pallas_call(
            kernel,
            name=name,
            grid=(HEADS,),
            out_shape=shape(token_rows, width) if last else sums,
            in_specs=[smem, head(token_rows)] + specs + (sum_specs if stats else []),
            out_specs=head(token_rows) if last else sum_specs,
            scratch_shapes=[pltpu.VMEM((head_size // 128, 128, 128), jnp.float32)] if last else [],
            compiler_params=params,
            cost_estimate=pl.CostEstimate(
                flops=4 * pairs * head_size, transcendentals=pairs, bytes_accessed=12 << 20
            ),
        )(me, query_rows, *arrays, *stats)

    stats = attention(
        near_kernel,
        "near",
        1152,
        [(key_rows, value_rows), l1, i1r],
        (),
    )
    edge_r, l4, stats = lax.optimization_barrier((edge_r, l4, stats))
    via_r = edge_r
    if detours:
        via_r = lax.ppermute(edge_r, "ctx", [(via, t) for (_, t), via in detours.items()])
    steps = [shifts for shifts in flow_spans if abs(shifts[0]) != 4]
    yrs += [lax.ppermute(l4, "ctx", flow_pairs(shifts, count)) for shifts in steps]
    x2r, yrs, stats = lax.optimization_barrier((x2r, yrs, stats))
    tables = [x2r, lax.ppermute(x2r, "ctx", mates)]
    for yr in yrs:
        tables += [yr, lax.ppermute(yr, "ctx", mates)]
    edge_r, via_r, x1r, tables = lax.optimization_barrier((edge_r, via_r, x1r, tables))
    xt, i2s = pl.pallas_call(
        functools.partial(rim_kernel, [t for _, t in detours]),
        name="rim",
        grid=(2,),
        out_shape=[shape(TABLE_ROWS), shape(256)],
        in_specs=[smem, column(EDGE_ROWS), column(EDGE_ROWS), column(RIM_ROWS)],
        out_specs=[column(TABLE_ROWS), column(256)],
        scratch_shapes=[pltpu.VMEM((cut // 128, 384, 128), jnp.float32)],
        compiler_params=params,
    )(me, edge_r, via_r, x1r)
    i2r = lax.ppermute(i2s, "ctx", mates)
    kernel = functools.partial(far_kernel, flow_spans, count)
    return attention(kernel, "far", 1088, [xt, i2r] + tables, stats, True)


def solution(mesh):
    spec = P(("dp", "ctx"), None)
    return jax.shard_map(
        on_device, mesh=mesh, in_specs=(spec, spec, spec), out_specs=spec, check_vma=False
    )
```

```python
import functools
import math

import jax
import jax.numpy as jnp
import ml_dtypes
import numpy as np
from jax import lax
from jax.experimental import pallas as pl
from jax.experimental.pallas import tpu as pltpu
from jax.sharding import PartitionSpec as P

HEADS = 4
LEAF = 256
LEVELS = 5
HALF = LEAF // 2
BLOCKS = 4
EDGE_ROWS = 256
RIM_ROWS = 320
TABLE_ROWS = 896
L1_AT = 256
L2_AT = 640
FAR_ROWS = 192
HIDDEN = -1e30
SAFE_TOTAL = 2.0**100


def pooled(x, wide_ref):
    rows, width = x.shape
    parts = []
    for at in range(width // 128):
        wide_ref[at, 0:rows, :] = x[:, at * 128 : (at + 1) * 128].astype(jnp.float32)
        even = wide_ref[at, pl.ds(0, rows // 2, stride=2), :]
        odd = wide_ref[at, pl.ds(1, rows // 2, stride=2), :]
        parts.append(((even + odd) * 0.5).astype(x.dtype))
    return jnp.concatenate(parts, axis=1) if len(parts) > 1 else parts[0]


def pool_kernel(
    dev_ref, k_ref, v_ref, edge_ref, x1_ref, i1_ref, x2_ref, y_ref, l4_ref, l1_ref, wide_ref
):
    odd = dev_ref[0] % 2 == 1
    steps = pl.num_programs(0) // 2
    at = pl.program_id(0)

    def write(l0):
        l1 = pooled(l0[...], wide_ref)
        l2 = pooled(l1, wide_ref)
        l3 = pooled(l2, wide_ref)
        l4 = pooled(l3, wide_ref)
        l1_ref[...] = l1
        y_ref[0:128, :] = l3
        y_ref[128:192, :] = l4
        l4_ref[...] = l4
        i1_ref[L2_AT:TABLE_ROWS, :] = l2

        @pl.when(odd)
        def _():
            edge_ref[...] = l0[768:1024, :]
            x1_ref[0:128, :] = l1[256:384]
            x1_ref[128:256, :] = l2[0:128]
            x1_ref[256:320, :] = l2[0:64]
            i1_ref[0:256, :] = l0[0:256, :]
            i1_ref[L1_AT:L2_AT, :] = l1[0:384]
            x2_ref[0:128, :] = l2[0:128]
            x2_ref[128:192, :] = l3[64:128]

        @pl.when(jnp.logical_not(odd))
        def _():
            edge_ref[...] = l0[0:256, :]
            x1_ref[0:256, :] = l1[128:384]
            x1_ref[256:320, :] = l2[192:256]
            i1_ref[0:256, :] = l0[768:1024, :]
            i1_ref[L1_AT : L1_AT + 256, :] = l1[256:512]
            i1_ref[L1_AT + 256 : L2_AT, :] = l1[0:128]
            x2_ref[0:128, :] = l3
            x2_ref[128:192, :] = l3[64:128]

    @pl.when(at < steps)
    def _():
        write(k_ref)

    @pl.when(at >= steps)
    def _():
        write(v_ref)


def rim_kernel(relayed, dev_ref, edge_ref, via_ref, x1_ref, xt_ref, i2_ref, wide_ref):
    me = dev_ref[0]
    odd = me % 2 == 1
    if relayed:
        twice = functools.reduce(jnp.logical_or, [me == target for target in relayed])

        @pl.when(twice)
        def _():
            xt_ref[0:256, :] = via_ref[...]

        @pl.when(jnp.logical_not(twice))
        def _():
            xt_ref[0:256, :] = edge_ref[...]
    else:
        xt_ref[0:256, :] = edge_ref[...]

    @pl.when(odd)
    def _():
        l1 = jnp.concatenate([pooled(xt_ref[0:256, :], wide_ref), x1_ref[0:256, :]], axis=0)
        l2 = jnp.concatenate([pooled(l1, wide_ref), x1_ref[256:320, :]], axis=0)
        xt_ref[L1_AT:L2_AT, :] = l1
        xt_ref[L2_AT:TABLE_ROWS, :] = l2
        i2_ref[0:128, :] = l2[0:128]
        i2_ref[128:256, :] = pooled(l2, wide_ref)

    @pl.when(jnp.logical_not(odd))
    def _():
        l1 = jnp.concatenate([x1_ref[0:128, :], pooled(xt_ref[0:256, :], wide_ref)], axis=0)
        l2 = jnp.concatenate([x1_ref[128:256, :], pooled(l1, wide_ref)], axis=0)
        xt_ref[L1_AT : L1_AT + 256, :] = l1
        xt_ref[L1_AT + 256 : L2_AT, :] = l1[0:128]
        xt_ref[L2_AT:TABLE_ROWS, :] = l2
        l3 = pooled(l2, wide_ref)
        i2_ref[0:128, :] = l3
        i2_ref[128:256, :] = l3


def offset_lanes(level, valid, scale):
    terms = []
    rest = level / scale
    for _ in range(3):
        term = float(np.float32(rest).astype(ml_dtypes.bfloat16))
        terms.append(term)
        rest -= term
    if valid is not None:
        terms = [jnp.where(valid, t, h) for t, h in zip(terms, (HIDDEN, 0.0, 0.0))]
    lane = lax.broadcasted_iota(jnp.int32, (128, 128), 1)
    lanes = jnp.zeros((128, 128), jnp.float32)
    for at, term in enumerate(terms):
        lanes = jnp.where(lane == at, term, lanes)
    return lanes.astype(jnp.bfloat16)


def chunks_of(segments):
    chunks = [[]]
    room = 256
    for k_ref, v_ref, start, count, lanes in segments:
        while count:
            take = min(count, room, 128)
            chunks[-1].append((k_ref, v_ref, start, take, lanes))
            start, count, room = start + take, count - take, room - take
            if not room:
                chunks.append([])
                room = 256
    return [chunk for chunk in chunks if chunk]


def attend(query, segments, scale, before, exact):
    rows = query.shape[0]
    lane = lax.broadcasted_iota(jnp.int32, query.shape, 1)
    query = jnp.concatenate([query, jnp.where(lane < 3, 1.0, 0.0).astype(query.dtype)], axis=1)
    chunks = chunks_of(segments)
    scores = []
    peak = None
    for chunk in chunks:
        keys = jnp.concatenate(
            [
                jnp.concatenate([k_ref[start : start + count, :], lanes[0:count]], axis=1)
                for k_ref, _, start, count, lanes in chunk
            ],
            axis=0,
        )
        score = lax.dot_general(
            query, keys, (((1,), (1,)), ((), ())), preferred_element_type=jnp.float32
        )
        scores.append(score)
        if not exact and (peak is not None or before is not None):
            continue
        for col in range(0, keys.shape[0], 128):
            top = score[:, col : col + 128]
            peak = top if peak is None else jnp.maximum(peak, top)
    if peak is None:
        peak = before
    else:
        peak = jnp.max(peak, axis=1, keepdims=True) * scale
        if before is not None:
            peak = jnp.maximum(peak, before)
    out = None
    for chunk, score in zip(chunks, scores):
        weight = jnp.exp2(score * scale - peak).astype(jnp.bfloat16)
        values = jnp.concatenate(
            [v_ref[start : start + count, :] for _, v_ref, start, count, _ in chunk], axis=0
        )
        table = jnp.concatenate([values, jnp.ones((values.shape[0], 128), jnp.bfloat16)], axis=1)
        part = jnp.dot(weight, table, preferred_element_type=jnp.float32)
        out = part if out is None else out + part
    return peak, out[:, 0:128], out[:, 128:256]


def base_two_scale(head_size):
    return math.log2(math.e) / math.sqrt(head_size)


def near_kernel(dev_ref, q_ref, k_ref, v_ref, l1k, l1v, mk, mv, *sums):
    scale = base_two_scale(q_ref.shape[1])
    zero = offset_lanes(0, None, scale)
    one = offset_lanes(1, None, scale)
    two = offset_lanes(2, None, scale)
    own = ((256, 256), None, (0, 128), (0, 256))

    def run(odd):
        if odd:
            mate = (
                [(mk, mv, 0, 256, zero), (mk, mv, L1_AT, 128, one), (mk, mv, L2_AT, 128, two)],
                [(mk, mv, L1_AT, 256, one), (mk, mv, L2_AT, 128, two)],
                [(mk, mv, L2_AT, 256, two)],
                [(mk, mv, L2_AT, 256, two)],
            )
        else:
            mate = (
                [(mk, mv, L2_AT, 256, two)],
                [(mk, mv, L1_AT, 128, one), (mk, mv, L2_AT, 256, two)],
                [(mk, mv, L1_AT, 256, one)],
                [(mk, mv, 0, 256, zero), (mk, mv, L1_AT + 256, 128, one)],
            )
        def one_block(block, exact):
            low, high = max(block - 1, 0), min(block + 2, BLOCKS)
            segments = [(k_ref, v_ref, low * LEAF, (high - low) * LEAF, zero)]
            if own[block]:
                segments.append((l1k, l1v, own[block][0], own[block][1], one))
            here = slice(block * LEAF, (block + 1) * LEAF)
            peak, acc, total = attend(q_ref[here, :], segments + mate[block], scale, None, exact)
            write_sums(sums, here, peak, acc, total)
            return total

        all_blocks(one_block)

    @pl.when(dev_ref[0] % 2 == 1)
    def _():
        run(True)

    @pl.when(dev_ref[0] % 2 == 0)
    def _():
        run(False)


def read_mass(mass_ref, here):
    packed = mass_ref[here, :]
    lane = lax.broadcasted_iota(jnp.int32, packed.shape, 1)
    own = jnp.where(lane == pl.program_id(0), packed, 0.0)
    return jnp.sum(own, axis=1, keepdims=True)


def write_sums(sums, here, peak, acc, total):
    mean_ref, mass_ref = sums
    mean_ref[here, :] = acc / total
    lane = lax.broadcasted_iota(jnp.int32, acc.shape, 1)
    mass = peak + jnp.log2(total)
    kept = jnp.where(pl.program_id(0) == 0, 0.0, mass_ref[here, :])
    mass_ref[here, :] = jnp.where(lane == pl.program_id(0), mass, kept)


def all_blocks(one_block):
    largest = None
    for block in range(BLOCKS):
        total = one_block(block, False)
        largest = total if largest is None else jnp.maximum(largest, total)

    @pl.when(jnp.logical_not(jnp.max(largest) < SAFE_TOTAL))
    def _():
        for block in range(BLOCKS):
            one_block(block, True)


def attend_after(query, segments, scale, stats, here, exact):
    mean_ref, mass_ref = stats
    mass = read_mass(mass_ref, here)
    peak, acc, total = attend(query, segments, scale, mass, exact)
    if not exact:
        return peak, mean_ref[here, :] + acc, total + 1.0
    factor = jnp.exp2(mass - peak)
    return peak, mean_ref[here, :] * factor + acc, total + factor


def far_kernel(flow_spans, count, dev_ref, q_ref, *refs):
    xk, xv, i2k, i2v, x2k, x2v, x2mk, x2mv = refs[0:8]
    stats, out_ref, wide_ref = refs[-4:-2], refs[-2], refs[-1]
    flow_refs = [refs[8 + 4 * at : 12 + 4 * at] for at in range(len(flow_spans))]
    scale = base_two_scale(q_ref.shape[1])
    me = dev_ref[0]
    chip = me // 2
    chips = count // 2

    def lanes(level, valid):
        return offset_lanes(level, valid, scale)

    quads = []
    for shifts, (yk, yv, ymk, ymv) in zip(flow_spans, flow_refs):
        valid = False
        for shift in shifts:
            source = chip - shift // 2
            here = (source >= 0) & (source < chips)
            if shift == -4:
                here = here & (chip % 2 == 0)
            if shift == 6:
                here = here & (chip % 2 == 1)
            valid = here | valid
        four = lanes(4, valid)
        start = yk.shape[0] - 64
        quads += [(yk, yv, start, 64, four), (ymk, ymv, start, 64, four)]

    def run(odd):
        near = (me < count - 1) if odd else (me >= 1)
        zero, one, two = (lanes(level, near) for level in range(3))
        beyond = lanes(2, me + 2 < count)
        if odd:
            ymk, ymv = flow_refs[0][2:4]
            coarse = [
                (ymk, ymv, 0, 128, lanes(3, me + 3 < count)),
                (x2k, x2v, 0, 128, lanes(3, me - 3 >= 0)),
                (i2k, i2v, 0, 128, lanes(3, me - 2 >= 0)),
            ]
            skip = (x2mk, x2mv, 0, 128, beyond)
            rim = (
                [(xk, xv, L2_AT, 256, two)],
                [(xk, xv, L2_AT, 256, two), (xk, xv, L1_AT, 128, one)],
                [(xk, xv, L1_AT, 256, one), skip],
                [(xk, xv, 0, 256, zero), (xk, xv, L1_AT + 256, 128, one), skip],
            )
        else:
            third = [
                jnp.concatenate([pooled(table[0:128, :], wide_ref), table[128:192, :]], axis=0)
                for table in (x2k, x2v)
            ]
            coarse = [
                (x2mk, x2mv, 0, 128, lanes(3, me - 2 >= 0)),
                (third[0], third[1], 0, 128, lanes(3, me + 3 < count)),
                (i2k, i2v, 128, 128, lanes(3, me + 2 < count)),
            ]
            skip = (i2k, i2v, 0, 128, beyond)
            rim = (
                [(xk, xv, 0, 256, zero), (xk, xv, L1_AT, 128, one), (xk, xv, L2_AT, 128, two)],
                [(xk, xv, L1_AT, 256, one), (xk, xv, L2_AT, 128, two)],
                [(xk, xv, L2_AT, 256, two), skip],
                [(xk, xv, L2_AT, 256, two), skip],
            )
        def one_block(block, exact):
            here = slice(block * LEAF, (block + 1) * LEAF)
            segments = quads + coarse[0:2] + rim[block] + coarse[2:3]
            _, acc, total = attend_after(q_ref[here, :], segments, scale, stats, here, exact)
            out_ref[here, :] = (acc / total).astype(out_ref.dtype)
            return total

        all_blocks(one_block)

    @pl.when(me % 2 == 1)
    def _():
        run(True)

    @pl.when(me % 2 == 0)
    def _():
        run(False)


def relays(count):
    return {(3, 4): 7, (4, 3): 0} if count == 8 else {}


def flow_pairs(shifts, count):
    pairs = []
    for shift in shifts:
        for source in range(count):
            target = source + shift
            if 0 <= target < count and not (shift == 6 and target // 2 % 2 == 0):
                pairs.append((source, target))
    return pairs


def far_flows(count):
    spans = []
    for low, high in ((-4, 4), (-6, 6)):
        pairs = flow_pairs((low, high), count)
        unique = len({s for s, _ in pairs}) == len(pairs) == len({t for _, t in pairs})
        spans.extend([(low, high)] if unique else [(low,), (high,)])
    return tuple(spans)


def on_device(query_rows, key_rows, value_rows):
    token_rows, width = query_rows.shape
    head_size = width // HEADS
    count = lax.axis_size("ctx")
    me = lax.axis_index("ctx").astype(jnp.int32).reshape(1)
    dtype = key_rows.dtype

    def shape(rows, columns=2 * width, kind=dtype):
        return jax.ShapeDtypeStruct((rows, columns), kind)

    smem = pl.BlockSpec(memory_space=pltpu.SMEM)
    params = pltpu.CompilerParams(vmem_limit_bytes=64 << 20)

    near = range(1, count - 1, 2)
    across = [(i, i + 1) for i in near] + [(i + 1, i) for i in near]
    detours = relays(count)
    cut = width

    def column(rows):
        return pl.BlockSpec((rows, cut), lambda j: (0, j))

    pooled_rows = (EDGE_ROWS, RIM_ROWS, TABLE_ROWS, FAR_ROWS, 192, 64, token_rows // 2)
    edge, x1s, i1s, x2s, ys, l4, l1 = pl.pallas_call(
        pool_kernel,
        name="pool",
        grid=(2,),
        out_shape=[shape(rows) for rows in pooled_rows],
        in_specs=[
            smem,
            pl.BlockSpec((token_rows, cut), lambda j: (0, 0)),
            pl.BlockSpec((token_rows, cut), lambda j: (0, 0)),
        ],
        out_specs=[column(rows) for rows in pooled_rows],
        scratch_shapes=[pltpu.VMEM((cut // 128, token_rows, 128), jnp.float32)],
        compiler_params=params,
        cost_estimate=pl.CostEstimate(flops=0, transcendentals=0, bytes_accessed=24 << 20),
    )(me, key_rows, value_rows)

    edge_r = lax.ppermute(edge, "ctx", [(s, detours.get((s, t), t)) for s, t in across])
    x2r = lax.ppermute(
        x2s,
        "ctx",
        [(i, i + 3) for i in range(0, count - 3, 2)] + [(i, i - 3) for i in range(3, count, 2)],
    )
    flow_spans = far_flows(count)
    yrs = [
        lax.ppermute(ys if abs(shifts[0]) == 4 else l4, "ctx", flow_pairs(shifts, count))
        for shifts in flow_spans
    ]
    x1r = lax.ppermute(x1s, "ctx", across)
    mates = [(i, i ^ 1) for i in range(count)]
    i1r = lax.ppermute(i1s, "ctx", mates)

    def head(rows, base=0):
        return pl.BlockSpec((rows, head_size), lambda h, *_: (0, base + h))

    def attention(kernel, name, keys, tables, stats, last=False):
        arrays, specs = [], []
        for table in tables:
            if isinstance(table, tuple):
                arrays += table
                specs += [head(table[0].shape[0])] * 2
            else:
                arrays += [table, table]
                specs += [head(table.shape[0]), head(table.shape[0], HEADS)]
        pairs = token_rows * keys * HEADS
        sums = [shape(token_rows, width, jnp.float32), shape(token_rows, 128, jnp.float32)]
        sum_specs = [head(token_rows), pl.BlockSpec((token_rows, 128), lambda h: (0, 0))]
        return pl.pallas_call(
            kernel,
            name=name,
            grid=(HEADS,),
            out_shape=shape(token_rows, width) if last else sums,
            in_specs=[smem, head(token_rows)] + specs + (sum_specs if stats else []),
            out_specs=head(token_rows) if last else sum_specs,
            scratch_shapes=[pltpu.VMEM((head_size // 128, 128, 128), jnp.float32)] if last else [],
            compiler_params=params,
            cost_estimate=pl.CostEstimate(
                flops=4 * pairs * head_size, transcendentals=pairs, bytes_accessed=12 << 20
            ),
        )(me, query_rows, *arrays, *stats)

    stats = attention(
        near_kernel,
        "near",
        1152,
        [(key_rows, value_rows), l1, i1r],
        (),
    )
    edge_r, stats = lax.optimization_barrier((edge_r, stats))
    via_r = edge_r
    if detours:
        via_r = lax.ppermute(edge_r, "ctx", [(via, t) for (_, t), via in detours.items()])
    x2r, yrs, stats = lax.optimization_barrier((x2r, yrs, stats))
    tables = [x2r, lax.ppermute(x2r, "ctx", mates)]
    for yr in yrs:
        tables += [yr, lax.ppermute(yr, "ctx", mates)]
    edge_r, via_r, x1r, tables = lax.optimization_barrier((edge_r, via_r, x1r, tables))
    xt, i2s = pl.pallas_call(
        functools.partial(rim_kernel, [t for _, t in detours]),
        name="rim",
        grid=(2,),
        out_shape=[shape(TABLE_ROWS), shape(256)],
        in_specs=[smem, column(EDGE_ROWS), column(EDGE_ROWS), column(RIM_ROWS)],
        out_specs=[column(TABLE_ROWS), column(256)],
        scratch_shapes=[pltpu.VMEM((cut // 128, 384, 128), jnp.float32)],
        compiler_params=params,
    )(me, edge_r, via_r, x1r)
    i2r = lax.ppermute(i2s, "ctx", mates)
    kernel = functools.partial(far_kernel, flow_spans, count)
    return attention(kernel, "far", 1088, [xt, i2r] + tables, stats, True)


def solution(mesh):
    spec = P(("dp", "ctx"), None)
    return jax.shard_map(
        on_device, mesh=mesh, in_specs=(spec, spec, spec), out_specs=spec, check_vma=False
    )
```

```python
import functools
import math

import jax
import jax.numpy as jnp
import ml_dtypes
import numpy as np
from jax import lax
from jax.experimental import pallas as pl
from jax.experimental.pallas import tpu as pltpu
from jax.sharding import PartitionSpec as P

HEADS = 4
LEAF = 256
LEVELS = 5
HALF = LEAF // 2
BLOCKS = 4
EDGE_ROWS = 256
RIM_ROWS = 320
TABLE_ROWS = 896
L1_AT = 256
L2_AT = 640
FAR_ROWS = 192
HIDDEN = -1e30
SAFE_TOTAL = 2.0**100


def pooled(x, wide_ref):
    rows, width = x.shape
    parts = []
    for at in range(width // 128):
        wide_ref[at, 0:rows, :] = x[:, at * 128 : (at + 1) * 128].astype(jnp.float32)
        even = wide_ref[at, pl.ds(0, rows // 2, stride=2), :]
        odd = wide_ref[at, pl.ds(1, rows // 2, stride=2), :]
        parts.append(((even + odd) * 0.5).astype(x.dtype))
    return jnp.concatenate(parts, axis=1) if len(parts) > 1 else parts[0]


def pool_kernel(
    dev_ref, k_ref, v_ref, edge_ref, x1_ref, i1_ref, x2_ref, y_ref, l4_ref, l1_ref, wide_ref
):
    odd = dev_ref[0] % 2 == 1
    steps = pl.num_programs(0) // 2
    at = pl.program_id(0)

    def write(l0):
        l1 = pooled(l0[...], wide_ref)
        l2 = pooled(l1, wide_ref)
        l3 = pooled(l2, wide_ref)
        l4 = pooled(l3, wide_ref)
        l1_ref[...] = l1
        y_ref[0:128, :] = l3
        y_ref[128:192, :] = l4
        l4_ref[...] = l4
        i1_ref[L2_AT:TABLE_ROWS, :] = l2

        @pl.when(odd)
        def _():
            edge_ref[...] = l0[768:1024, :]
            x1_ref[0:128, :] = l1[256:384]
            x1_ref[128:256, :] = l2[0:128]
            x1_ref[256:320, :] = l2[0:64]
            i1_ref[0:256, :] = l0[0:256, :]
            i1_ref[L1_AT:L2_AT, :] = l1[0:384]
            x2_ref[0:128, :] = l2[0:128]
            x2_ref[128:192, :] = l3[64:128]

        @pl.when(jnp.logical_not(odd))
        def _():
            edge_ref[...] = l0[0:256, :]
            x1_ref[0:256, :] = l1[128:384]
            x1_ref[256:320, :] = l2[192:256]
            i1_ref[0:256, :] = l0[768:1024, :]
            i1_ref[L1_AT : L1_AT + 256, :] = l1[256:512]
            i1_ref[L1_AT + 256 : L2_AT, :] = l1[0:128]
            x2_ref[0:128, :] = l3
            x2_ref[128:192, :] = l3[64:128]

    @pl.when(at < steps)
    def _():
        write(k_ref)

    @pl.when(at >= steps)
    def _():
        write(v_ref)


def rim_kernel(relayed, dev_ref, edge_ref, via_ref, x1_ref, xt_ref, i2_ref, wide_ref):
    me = dev_ref[0]
    odd = me % 2 == 1
    if relayed:
        twice = functools.reduce(jnp.logical_or, [me == target for target in relayed])

        @pl.when(twice)
        def _():
            xt_ref[0:256, :] = via_ref[...]

        @pl.when(jnp.logical_not(twice))
        def _():
            xt_ref[0:256, :] = edge_ref[...]
    else:
        xt_ref[0:256, :] = edge_ref[...]

    @pl.when(odd)
    def _():
        l1 = jnp.concatenate([pooled(xt_ref[0:256, :], wide_ref), x1_ref[0:256, :]], axis=0)
        l2 = jnp.concatenate([pooled(l1, wide_ref), x1_ref[256:320, :]], axis=0)
        xt_ref[L1_AT:L2_AT, :] = l1
        xt_ref[L2_AT:TABLE_ROWS, :] = l2
        i2_ref[0:128, :] = l2[0:128]
        i2_ref[128:256, :] = pooled(l2, wide_ref)

    @pl.when(jnp.logical_not(odd))
    def _():
        l1 = jnp.concatenate([x1_ref[0:128, :], pooled(xt_ref[0:256, :], wide_ref)], axis=0)
        l2 = jnp.concatenate([x1_ref[128:256, :], pooled(l1, wide_ref)], axis=0)
        xt_ref[L1_AT : L1_AT + 256, :] = l1
        xt_ref[L1_AT + 256 : L2_AT, :] = l1[0:128]
        xt_ref[L2_AT:TABLE_ROWS, :] = l2
        l3 = pooled(l2, wide_ref)
        i2_ref[0:128, :] = l3
        i2_ref[128:256, :] = l3


def offset_lanes(level, valid, scale):
    terms = []
    rest = level / scale
    for _ in range(3):
        term = float(np.float32(rest).astype(ml_dtypes.bfloat16))
        terms.append(term)
        rest -= term
    if valid is not None:
        terms = [jnp.where(valid, t, h) for t, h in zip(terms, (HIDDEN, 0.0, 0.0))]
    lane = lax.broadcasted_iota(jnp.int32, (128, 128), 1)
    lanes = jnp.zeros((128, 128), jnp.float32)
    for at, term in enumerate(terms):
        lanes = jnp.where(lane == at, term, lanes)
    return lanes.astype(jnp.bfloat16)


def chunks_of(segments):
    chunks = [[]]
    room = 256
    for k_ref, v_ref, start, count, lanes in segments:
        while count:
            take = min(count, room, 128)
            chunks[-1].append((k_ref, v_ref, start, take, lanes))
            start, count, room = start + take, count - take, room - take
            if not room:
                chunks.append([])
                room = 256
    return [chunk for chunk in chunks if chunk]


def attend(query, segments, scale, before, exact):
    rows = query.shape[0]
    lane = lax.broadcasted_iota(jnp.int32, query.shape, 1)
    query = jnp.concatenate([query, jnp.where(lane < 3, 1.0, 0.0).astype(query.dtype)], axis=1)
    chunks = chunks_of(segments)
    scores = []
    peak = None
    for chunk in chunks:
        keys = jnp.concatenate(
            [
                jnp.concatenate([k_ref[start : start + count, :], lanes[0:count]], axis=1)
                for k_ref, _, start, count, lanes in chunk
            ],
            axis=0,
        )
        score = lax.dot_general(
            query, keys, (((1,), (1,)), ((), ())), preferred_element_type=jnp.float32
        )
        scores.append(score)
        if not exact and (peak is not None or before is not None):
            continue
        for col in range(0, keys.shape[0], 128):
            top = score[:, col : col + 128]
            peak = top if peak is None else jnp.maximum(peak, top)
    if peak is None:
        peak = before
    else:
        peak = jnp.max(peak, axis=1, keepdims=True) * scale
        if before is not None:
            peak = jnp.maximum(peak, before)
    out = None
    for chunk, score in zip(chunks, scores):
        weight = jnp.exp2(score * scale - peak).astype(jnp.bfloat16)
        values = jnp.concatenate(
            [v_ref[start : start + count, :] for _, v_ref, start, count, _ in chunk], axis=0
        )
        table = jnp.concatenate([values, jnp.ones((values.shape[0], 128), jnp.bfloat16)], axis=1)
        part = jnp.dot(weight, table, preferred_element_type=jnp.float32)
        out = part if out is None else out + part
    return peak, out[:, 0:128], out[:, 128:256]


def base_two_scale(head_size):
    return math.log2(math.e) / math.sqrt(head_size)


def near_kernel(dev_ref, q_ref, k_ref, v_ref, l1k, l1v, mk, mv, *sums):
    scale = base_two_scale(q_ref.shape[1])
    zero = offset_lanes(0, None, scale)
    one = offset_lanes(1, None, scale)
    two = offset_lanes(2, None, scale)
    own = ((256, 256), None, (0, 128), (0, 256))

    def run(odd):
        if odd:
            mate = (
                [(mk, mv, 0, 256, zero), (mk, mv, L1_AT, 128, one), (mk, mv, L2_AT, 128, two)],
                [(mk, mv, L1_AT, 256, one), (mk, mv, L2_AT, 128, two)],
                [(mk, mv, L2_AT, 256, two)],
                [(mk, mv, L2_AT, 256, two)],
            )
        else:
            mate = (
                [(mk, mv, L2_AT, 256, two)],
                [(mk, mv, L1_AT, 128, one), (mk, mv, L2_AT, 256, two)],
                [(mk, mv, L1_AT, 256, one)],
                [(mk, mv, 0, 256, zero), (mk, mv, L1_AT + 256, 128, one)],
            )
        def one_block(block, exact):
            low, high = max(block - 1, 0), min(block + 2, BLOCKS)
            segments = [(k_ref, v_ref, low * LEAF, (high - low) * LEAF, zero)]
            if own[block]:
                segments.append((l1k, l1v, own[block][0], own[block][1], one))
            here = slice(block * LEAF, (block + 1) * LEAF)
            peak, acc, total = attend(q_ref[here, :], segments + mate[block], scale, None, exact)
            write_sums(sums, here, peak, acc, total)
            return total

        all_blocks(one_block)

    @pl.when(dev_ref[0] % 2 == 1)
    def _():
        run(True)

    @pl.when(dev_ref[0] % 2 == 0)
    def _():
        run(False)


def read_mass(mass_ref, here):
    packed = mass_ref[here, :]
    lane = lax.broadcasted_iota(jnp.int32, packed.shape, 1)
    own = jnp.where(lane == pl.program_id(0), packed, 0.0)
    return jnp.sum(own, axis=1, keepdims=True)


def write_sums(sums, here, peak, acc, total):
    mean_ref, mass_ref = sums
    mean_ref[here, :] = acc / total
    lane = lax.broadcasted_iota(jnp.int32, acc.shape, 1)
    mass = peak + jnp.log2(total)
    kept = jnp.where(pl.program_id(0) == 0, 0.0, mass_ref[here, :])
    mass_ref[here, :] = jnp.where(lane == pl.program_id(0), mass, kept)


def all_blocks(one_block):
    largest = None
    for block in range(BLOCKS):
        total = jnp.max(one_block(block, False), axis=0, keepdims=True)
        largest = total if largest is None else jnp.maximum(largest, total)

    @pl.when(jnp.logical_not(largest[0, 0] < SAFE_TOTAL))
    def _():
        for block in range(BLOCKS):
            one_block(block, True)


def attend_after(query, segments, scale, stats, here, exact):
    mean_ref, mass_ref = stats
    mass = read_mass(mass_ref, here)
    peak, acc, total = attend(query, segments, scale, mass, exact)
    if not exact:
        return peak, mean_ref[here, :] + acc, total + 1.0
    factor = jnp.exp2(mass - peak)
    return peak, mean_ref[here, :] * factor + acc, total + factor


def far_kernel(flow_spans, count, dev_ref, q_ref, *refs):
    xk, xv, i2k, i2v, x2k, x2v, x2mk, x2mv = refs[0:8]
    stats, out_ref, wide_ref = refs[-4:-2], refs[-2], refs[-1]
    flow_refs = [refs[8 + 4 * at : 12 + 4 * at] for at in range(len(flow_spans))]
    scale = base_two_scale(q_ref.shape[1])
    me = dev_ref[0]
    chip = me // 2
    chips = count // 2

    def lanes(level, valid):
        return offset_lanes(level, valid, scale)

    quads = []
    for shifts, (yk, yv, ymk, ymv) in zip(flow_spans, flow_refs):
        valid = False
        for shift in shifts:
            source = chip - shift // 2
            here = (source >= 0) & (source < chips)
            if shift == -4:
                here = here & (chip % 2 == 0)
            if shift == 6:
                here = here & (chip % 2 == 1)
            valid = here | valid
        four = lanes(4, valid)
        start = yk.shape[0] - 64
        quads += [(yk, yv, start, 64, four), (ymk, ymv, start, 64, four)]

    def run(odd):
        near = (me < count - 1) if odd else (me >= 1)
        zero, one, two = (lanes(level, near) for level in range(3))
        beyond = lanes(2, me + 2 < count)
        if odd:
            ymk, ymv = flow_refs[0][2:4]
            coarse = [
                (ymk, ymv, 0, 128, lanes(3, me + 3 < count)),
                (x2k, x2v, 0, 128, lanes(3, me - 3 >= 0)),
                (i2k, i2v, 0, 128, lanes(3, me - 2 >= 0)),
            ]
            skip = (x2mk, x2mv, 0, 128, beyond)
            rim = (
                [(xk, xv, L2_AT, 256, two)],
                [(xk, xv, L2_AT, 256, two), (xk, xv, L1_AT, 128, one)],
                [(xk, xv, L1_AT, 256, one), skip],
                [(xk, xv, 0, 256, zero), (xk, xv, L1_AT + 256, 128, one), skip],
            )
        else:
            third = [
                jnp.concatenate([pooled(table[0:128, :], wide_ref), table[128:192, :]], axis=0)
                for table in (x2k, x2v)
            ]
            coarse = [
                (x2mk, x2mv, 0, 128, lanes(3, me - 2 >= 0)),
                (third[0], third[1], 0, 128, lanes(3, me + 3 < count)),
                (i2k, i2v, 128, 128, lanes(3, me + 2 < count)),
            ]
            skip = (i2k, i2v, 0, 128, beyond)
            rim = (
                [(xk, xv, 0, 256, zero), (xk, xv, L1_AT, 128, one), (xk, xv, L2_AT, 128, two)],
                [(xk, xv, L1_AT, 256, one), (xk, xv, L2_AT, 128, two)],
                [(xk, xv, L2_AT, 256, two), skip],
                [(xk, xv, L2_AT, 256, two), skip],
            )
        def one_block(block, exact):
            here = slice(block * LEAF, (block + 1) * LEAF)
            segments = quads + coarse[0:2] + rim[block] + coarse[2:3]
            _, acc, total = attend_after(q_ref[here, :], segments, scale, stats, here, exact)
            out_ref[here, :] = (acc / total).astype(out_ref.dtype)
            return total

        all_blocks(one_block)

    @pl.when(me % 2 == 1)
    def _():
        run(True)

    @pl.when(me % 2 == 0)
    def _():
        run(False)


def relays(count):
    return {(3, 4): 7, (4, 3): 0} if count == 8 else {}


def flow_pairs(shifts, count):
    pairs = []
    for shift in shifts:
        for source in range(count):
            target = source + shift
            if 0 <= target < count and not (shift == 6 and target // 2 % 2 == 0):
                pairs.append((source, target))
    return pairs


def far_flows(count):
    spans = []
    for low, high in ((-4, 4), (-6, 6)):
        pairs = flow_pairs((low, high), count)
        unique = len({s for s, _ in pairs}) == len(pairs) == len({t for _, t in pairs})
        spans.extend([(low, high)] if unique else [(low,), (high,)])
    return tuple(spans)


def on_device(query_rows, key_rows, value_rows):
    token_rows, width = query_rows.shape
    head_size = width // HEADS
    count = lax.axis_size("ctx")
    me = lax.axis_index("ctx").astype(jnp.int32).reshape(1)
    dtype = key_rows.dtype

    def shape(rows, columns=2 * width, kind=dtype):
        return jax.ShapeDtypeStruct((rows, columns), kind)

    smem = pl.BlockSpec(memory_space=pltpu.SMEM)
    params = pltpu.CompilerParams(vmem_limit_bytes=64 << 20)

    near = range(1, count - 1, 2)
    across = [(i, i + 1) for i in near] + [(i + 1, i) for i in near]
    detours = relays(count)
    cut = width

    def column(rows):
        return pl.BlockSpec((rows, cut), lambda j: (0, j))

    pooled_rows = (EDGE_ROWS, RIM_ROWS, TABLE_ROWS, FAR_ROWS, 192, 64, token_rows // 2)
    edge, x1s, i1s, x2s, ys, l4, l1 = pl.pallas_call(
        pool_kernel,
        name="pool",
        grid=(2,),
        out_shape=[shape(rows) for rows in pooled_rows],
        in_specs=[
            smem,
            pl.BlockSpec((token_rows, cut), lambda j: (0, 0)),
            pl.BlockSpec((token_rows, cut), lambda j: (0, 0)),
        ],
        out_specs=[column(rows) for rows in pooled_rows],
        scratch_shapes=[pltpu.VMEM((cut // 128, token_rows, 128), jnp.float32)],
        compiler_params=params,
        cost_estimate=pl.CostEstimate(flops=0, transcendentals=0, bytes_accessed=24 << 20),
    )(me, key_rows, value_rows)

    edge_r = lax.ppermute(edge, "ctx", [(s, detours.get((s, t), t)) for s, t in across])
    x2r = lax.ppermute(
        x2s,
        "ctx",
        [(i, i + 3) for i in range(0, count - 3, 2)] + [(i, i - 3) for i in range(3, count, 2)],
    )
    flow_spans = far_flows(count)
    yrs = [
        lax.ppermute(ys if abs(shifts[0]) == 4 else l4, "ctx", flow_pairs(shifts, count))
        for shifts in flow_spans
    ]
    x1r = lax.ppermute(x1s, "ctx", across)
    mates = [(i, i ^ 1) for i in range(count)]
    i1r = lax.ppermute(i1s, "ctx", mates)

    def head(rows, base=0):
        return pl.BlockSpec((rows, head_size), lambda h, *_: (0, base + h))

    def attention(kernel, name, keys, tables, stats, last=False):
        arrays, specs = [], []
        for table in tables:
            if isinstance(table, tuple):
                arrays += table
                specs += [head(table[0].shape[0])] * 2
            else:
                arrays += [table, table]
                specs += [head(table.shape[0]), head(table.shape[0], HEADS)]
        pairs = token_rows * keys * HEADS
        sums = [shape(token_rows, width, jnp.float32), shape(token_rows, 128, jnp.float32)]
        sum_specs = [head(token_rows), pl.BlockSpec((token_rows, 128), lambda h: (0, 0))]
        return pl.pallas_call(
            kernel,
            name=name,
            grid=(HEADS,),
            out_shape=shape(token_rows, width) if last else sums,
            in_specs=[smem, head(token_rows)] + specs + (sum_specs if stats else []),
            out_specs=head(token_rows) if last else sum_specs,
            scratch_shapes=[pltpu.VMEM((head_size // 128, 128, 128), jnp.float32)] if last else [],
            compiler_params=params,
            cost_estimate=pl.CostEstimate(
                flops=4 * pairs * head_size, transcendentals=pairs, bytes_accessed=12 << 20
            ),
        )(me, query_rows, *arrays, *stats)

    stats = attention(
        near_kernel,
        "near",
        1152,
        [(key_rows, value_rows), l1, i1r],
        (),
    )
    edge_r, stats = lax.optimization_barrier((edge_r, stats))
    via_r = edge_r
    if detours:
        via_r = lax.ppermute(edge_r, "ctx", [(via, t) for (_, t), via in detours.items()])
    x2r, yrs, stats = lax.optimization_barrier((x2r, yrs, stats))
    tables = [x2r, lax.ppermute(x2r, "ctx", mates)]
    for yr in yrs:
        tables += [yr, lax.ppermute(yr, "ctx", mates)]
    edge_r, via_r, x1r, tables = lax.optimization_barrier((edge_r, via_r, x1r, tables))
    xt, i2s = pl.pallas_call(
        functools.partial(rim_kernel, [t for _, t in detours]),
        name="rim",
        grid=(2,),
        out_shape=[shape(TABLE_ROWS), shape(256)],
        in_specs=[smem, column(EDGE_ROWS), column(EDGE_ROWS), column(RIM_ROWS)],
        out_specs=[column(TABLE_ROWS), column(256)],
        scratch_shapes=[pltpu.VMEM((cut // 128, 384, 128), jnp.float32)],
        compiler_params=params,
    )(me, edge_r, via_r, x1r)
    i2r = lax.ppermute(i2s, "ctx", mates)
    kernel = functools.partial(far_kernel, flow_spans, count)
    return attention(kernel, "far", 1088, [xt, i2r] + tables, stats, True)


def solution(mesh):
    spec = P(("dp", "ctx"), None)
    return jax.shard_map(
        on_device, mesh=mesh, in_specs=(spec, spec, spec), out_specs=spec, check_vma=False
    )
```

```python
import functools
import math

import jax
import jax.numpy as jnp
import ml_dtypes
import numpy as np
from jax import lax
from jax.experimental import pallas as pl
from jax.experimental.pallas import tpu as pltpu
from jax.sharding import PartitionSpec as P

HEADS = 4
LEAF = 256
LEVELS = 5
HALF = LEAF // 2
BLOCKS = 4
EDGE_ROWS = 256
RIM_ROWS = 320
TABLE_ROWS = 896
L1_AT = 256
L2_AT = 640
FAR_ROWS = 192
HIDDEN = -1e30
SAFE_TOTAL = 2.0**100


def pooled(x, wide_ref):
    rows, width = x.shape
    parts = []
    for at in range(width // 128):
        wide_ref[at, 0:rows, :] = x[:, at * 128 : (at + 1) * 128].astype(jnp.float32)
        even = wide_ref[at, pl.ds(0, rows // 2, stride=2), :]
        odd = wide_ref[at, pl.ds(1, rows // 2, stride=2), :]
        parts.append(((even + odd) * 0.5).astype(x.dtype))
    return jnp.concatenate(parts, axis=1) if len(parts) > 1 else parts[0]


def pool_kernel(
    dev_ref, k_ref, v_ref, edge_ref, x1_ref, i1_ref, x2_ref, y_ref, l4_ref, l1_ref, wide_ref
):
    odd = dev_ref[0] % 2 == 1
    steps = pl.num_programs(0) // 2
    at = pl.program_id(0)

    def write(l0):
        l1 = pooled(l0[...], wide_ref)
        l2 = pooled(l1, wide_ref)
        l3 = pooled(l2, wide_ref)
        l4 = pooled(l3, wide_ref)
        l1_ref[...] = l1
        y_ref[0:128, :] = l3
        y_ref[128:192, :] = l4
        l4_ref[...] = l4
        i1_ref[L2_AT:TABLE_ROWS, :] = l2

        @pl.when(odd)
        def _():
            edge_ref[...] = l0[768:1024, :]
            x1_ref[0:128, :] = l1[256:384]
            x1_ref[128:256, :] = l2[0:128]
            x1_ref[256:320, :] = l2[0:64]
            i1_ref[0:256, :] = l0[0:256, :]
            i1_ref[L1_AT:L2_AT, :] = l1[0:384]
            x2_ref[0:128, :] = l2[0:128]
            x2_ref[128:192, :] = l3[64:128]

        @pl.when(jnp.logical_not(odd))
        def _():
            edge_ref[...] = l0[0:256, :]
            x1_ref[0:256, :] = l1[128:384]
            x1_ref[256:320, :] = l2[192:256]
            i1_ref[0:256, :] = l0[768:1024, :]
            i1_ref[L1_AT : L1_AT + 256, :] = l1[256:512]
            i1_ref[L1_AT + 256 : L2_AT, :] = l1[0:128]
            x2_ref[0:128, :] = l3
            x2_ref[128:192, :] = l3[64:128]

    @pl.when(at < steps)
    def _():
        write(k_ref)

    @pl.when(at >= steps)
    def _():
        write(v_ref)


def rim_kernel(relayed, dev_ref, edge_ref, via_ref, x1_ref, xt_ref, i2_ref, wide_ref):
    me = dev_ref[0]
    odd = me % 2 == 1
    if relayed:
        twice = functools.reduce(jnp.logical_or, [me == target for target in relayed])

        @pl.when(twice)
        def _():
            xt_ref[0:256, :] = via_ref[...]

        @pl.when(jnp.logical_not(twice))
        def _():
            xt_ref[0:256, :] = edge_ref[...]
    else:
        xt_ref[0:256, :] = edge_ref[...]

    @pl.when(odd)
    def _():
        l1 = jnp.concatenate([pooled(xt_ref[0:256, :], wide_ref), x1_ref[0:256, :]], axis=0)
        l2 = jnp.concatenate([pooled(l1, wide_ref), x1_ref[256:320, :]], axis=0)
        xt_ref[L1_AT:L2_AT, :] = l1
        xt_ref[L2_AT:TABLE_ROWS, :] = l2
        i2_ref[0:128, :] = l2[0:128]
        i2_ref[128:256, :] = pooled(l2, wide_ref)

    @pl.when(jnp.logical_not(odd))
    def _():
        l1 = jnp.concatenate([x1_ref[0:128, :], pooled(xt_ref[0:256, :], wide_ref)], axis=0)
        l2 = jnp.concatenate([x1_ref[128:256, :], pooled(l1, wide_ref)], axis=0)
        xt_ref[L1_AT : L1_AT + 256, :] = l1
        xt_ref[L1_AT + 256 : L2_AT, :] = l1[0:128]
        xt_ref[L2_AT:TABLE_ROWS, :] = l2
        l3 = pooled(l2, wide_ref)
        i2_ref[0:128, :] = l3
        i2_ref[128:256, :] = l3


def offset_lanes(level, valid, scale):
    terms = []
    rest = level / scale
    for _ in range(3):
        term = float(np.float32(rest).astype(ml_dtypes.bfloat16))
        terms.append(term)
        rest -= term
    if valid is not None:
        terms = [jnp.where(valid, t, h) for t, h in zip(terms, (HIDDEN, 0.0, 0.0))]
    lane = lax.broadcasted_iota(jnp.int32, (128, 128), 1)
    lanes = jnp.zeros((128, 128), jnp.float32)
    for at, term in enumerate(terms):
        lanes = jnp.where(lane == at, term, lanes)
    return lanes.astype(jnp.bfloat16)


def chunks_of(segments):
    chunks = [[]]
    room = 256
    for k_ref, v_ref, start, count, lanes in segments:
        while count:
            take = min(count, room, 128)
            chunks[-1].append((k_ref, v_ref, start, take, lanes))
            start, count, room = start + take, count - take, room - take
            if not room:
                chunks.append([])
                room = 256
    return [chunk for chunk in chunks if chunk]


def attend(query, segments, scale, before, exact):
    rows = query.shape[0]
    lane = lax.broadcasted_iota(jnp.int32, query.shape, 1)
    query = jnp.concatenate([query, jnp.where(lane < 3, 1.0, 0.0).astype(query.dtype)], axis=1)
    chunks = chunks_of(segments)
    scores = []
    peak = None
    for chunk in chunks:
        keys = jnp.concatenate(
            [
                jnp.concatenate([k_ref[start : start + count, :], lanes[0:count]], axis=1)
                for k_ref, _, start, count, lanes in chunk
            ],
            axis=0,
        )
        score = lax.dot_general(
            query, keys, (((1,), (1,)), ((), ())), preferred_element_type=jnp.float32
        )
        scores.append(score)
        if not exact and (peak is not None or before is not None):
            continue
        for col in range(0, keys.shape[0], 128):
            top = score[:, col : col + 128]
            peak = top if peak is None else jnp.maximum(peak, top)
    if peak is None:
        peak = before
    else:
        peak = jnp.max(peak, axis=1, keepdims=True) * scale
        if before is not None:
            peak = jnp.maximum(peak, before)
    out = None
    for chunk, score in zip(chunks, scores):
        weight = jnp.exp2(score * scale - peak).astype(jnp.bfloat16)
        values = jnp.concatenate(
            [v_ref[start : start + count, :] for _, v_ref, start, count, _ in chunk], axis=0
        )
        table = jnp.concatenate([values, jnp.ones((values.shape[0], 128), jnp.bfloat16)], axis=1)
        part = jnp.dot(weight, table, preferred_element_type=jnp.float32)
        out = part if out is None else out + part
    return peak, out[:, 0:128], out[:, 128:256]


def base_two_scale(head_size):
    return math.log2(math.e) / math.sqrt(head_size)


def near_kernel(dev_ref, q_ref, k_ref, v_ref, l1k, l1v, mk, mv, *sums):
    scale = base_two_scale(q_ref.shape[1])
    zero = offset_lanes(0, None, scale)
    one = offset_lanes(1, None, scale)
    two = offset_lanes(2, None, scale)
    own = ((256, 256), None, (0, 128), (0, 256))

    def run(odd):
        if odd:
            mate = (
                [(mk, mv, 0, 256, zero), (mk, mv, L1_AT, 128, one), (mk, mv, L2_AT, 128, two)],
                [(mk, mv, L1_AT, 256, one), (mk, mv, L2_AT, 128, two)],
                [(mk, mv, L2_AT, 256, two)],
                [(mk, mv, L2_AT, 256, two)],
            )
        else:
            mate = (
                [(mk, mv, L2_AT, 256, two)],
                [(mk, mv, L1_AT, 128, one), (mk, mv, L2_AT, 256, two)],
                [(mk, mv, L1_AT, 256, one)],
                [(mk, mv, 0, 256, zero), (mk, mv, L1_AT + 256, 128, one)],
            )
        def one_block(block, exact):
            low, high = max(block - 1, 0), min(block + 2, BLOCKS)
            segments = [(k_ref, v_ref, low * LEAF, (high - low) * LEAF, zero)]
            if own[block]:
                segments.append((l1k, l1v, own[block][0], own[block][1], one))
            here = slice(block * LEAF, (block + 1) * LEAF)
            peak, acc, total = attend(q_ref[here, :], segments + mate[block], scale, None, exact)
            write_sums(sums, here, peak, acc, total)
            return total

        all_blocks(one_block)

    @pl.when(dev_ref[0] % 2 == 1)
    def _():
        run(True)

    @pl.when(dev_ref[0] % 2 == 0)
    def _():
        run(False)


def read_mass(mass_ref, here):
    packed = mass_ref[here, :]
    lane = lax.broadcasted_iota(jnp.int32, packed.shape, 1)
    own = jnp.where(lane == pl.program_id(0), packed, 0.0)
    return jnp.sum(own, axis=1, keepdims=True)


def write_sums(sums, here, peak, acc, total):
    mean_ref, mass_ref = sums
    mean_ref[here, :] = acc / total
    lane = lax.broadcasted_iota(jnp.int32, acc.shape, 1)
    mass = peak + jnp.log2(total)
    kept = jnp.where(pl.program_id(0) == 0, 0.0, mass_ref[here, :])
    mass_ref[here, :] = jnp.where(lane == pl.program_id(0), mass, kept)


def all_blocks(one_block):
    largest = None
    for block in range(BLOCKS):
        total = jnp.max(one_block(block, False), axis=0, keepdims=True)
        largest = total if largest is None else jnp.maximum(largest, total)

    @pl.when(jnp.logical_not(largest[0, 0] < SAFE_TOTAL))
    def _():
        for block in range(BLOCKS):
            one_block(block, True)


def attend_after(query, segments, scale, stats, here, exact):
    mean_ref, mass_ref = stats
    mass = read_mass(mass_ref, here)
    peak, acc, total = attend(query, segments, scale, mass, exact)
    if not exact:
        return peak, mean_ref[here, :] + acc, total + 1.0
    factor = jnp.exp2(mass - peak)
    return peak, mean_ref[here, :] * factor + acc, total + factor


def far_kernel(flow_spans, count, dev_ref, q_ref, *refs):
    xk, xv, i2k, i2v, x2k, x2v, x2mk, x2mv = refs[0:8]
    stats, out_ref, wide_ref = refs[-4:-2], refs[-2], refs[-1]
    flow_refs = [refs[8 + 4 * at : 12 + 4 * at] for at in range(len(flow_spans))]
    scale = base_two_scale(q_ref.shape[1])
    me = dev_ref[0]
    chip = me // 2
    chips = count // 2

    def lanes(level, valid):
        return offset_lanes(level, valid, scale)

    quads = []
    for shifts, (yk, yv, ymk, ymv) in zip(flow_spans, flow_refs):
        valid = False
        for shift in shifts:
            source = chip - shift // 2
            here = (source >= 0) & (source < chips)
            if shift == -4:
                here = here & (chip % 2 == 0)
            if shift == 6:
                here = here & (chip % 2 == 1)
            valid = here | valid
        four = lanes(4, valid)
        start = yk.shape[0] - 64
        quads += [(yk, yv, start, 64, four), (ymk, ymv, start, 64, four)]

    def run(odd):
        near = (me < count - 1) if odd else (me >= 1)
        zero, one, two = (lanes(level, near) for level in range(3))
        beyond = lanes(2, me + 2 < count)
        if odd:
            ymk, ymv = flow_refs[0][2:4]
            coarse = [
                (ymk, ymv, 0, 128, lanes(3, me + 3 < count)),
                (x2k, x2v, 0, 128, lanes(3, me - 3 >= 0)),
                (i2k, i2v, 0, 128, lanes(3, me - 2 >= 0)),
            ]
            skip = (x2mk, x2mv, 0, 128, beyond)
            rim = (
                [(xk, xv, L2_AT, 256, two)],
                [(xk, xv, L2_AT, 256, two), (xk, xv, L1_AT, 128, one)],
                [(xk, xv, L1_AT, 256, one), skip],
                [(xk, xv, 0, 256, zero), (xk, xv, L1_AT + 256, 128, one), skip],
            )
        else:
            third = [
                jnp.concatenate([pooled(table[0:128, :], wide_ref), table[128:192, :]], axis=0)
                for table in (x2k, x2v)
            ]
            coarse = [
                (x2mk, x2mv, 0, 128, lanes(3, me - 2 >= 0)),
                (third[0], third[1], 0, 128, lanes(3, me + 3 < count)),
                (i2k, i2v, 128, 128, lanes(3, me + 2 < count)),
            ]
            skip = (i2k, i2v, 0, 128, beyond)
            rim = (
                [(xk, xv, 0, 256, zero), (xk, xv, L1_AT, 128, one), (xk, xv, L2_AT, 128, two)],
                [(xk, xv, L1_AT, 256, one), (xk, xv, L2_AT, 128, two)],
                [(xk, xv, L2_AT, 256, two), skip],
                [(xk, xv, L2_AT, 256, two), skip],
            )
        def one_block(block, exact):
            here = slice(block * LEAF, (block + 1) * LEAF)
            segments = quads + coarse[0:2] + rim[block] + coarse[2:3]
            _, acc, total = attend_after(q_ref[here, :], segments, scale, stats, here, exact)
            out_ref[here, :] = (acc / total).astype(out_ref.dtype)
            return total

        all_blocks(one_block)

    @pl.when(me % 2 == 1)
    def _():
        run(True)

    @pl.when(me % 2 == 0)
    def _():
        run(False)


def relays(count):
    return {(3, 4): 7, (4, 3): 0} if count == 8 else {}


def flow_pairs(shifts, count):
    pairs = []
    for shift in shifts:
        for source in range(count):
            target = source + shift
            if 0 <= target < count and not (shift == 6 and target // 2 % 2 == 0):
                pairs.append((source, target))
    return pairs


def far_flows(count):
    spans = []
    for low, high in ((-4, 4), (-6, 6)):
        pairs = flow_pairs((low, high), count)
        unique = len({s for s, _ in pairs}) == len(pairs) == len({t for _, t in pairs})
        spans.extend([(low, high)] if unique else [(low,), (high,)])
    return tuple(spans)


def on_device(query_rows, key_rows, value_rows):
    token_rows, width = query_rows.shape
    head_size = width // HEADS
    count = lax.axis_size("ctx")
    me = lax.axis_index("ctx").astype(jnp.int32).reshape(1)
    dtype = key_rows.dtype

    def shape(rows, columns=2 * width, kind=dtype):
        return jax.ShapeDtypeStruct((rows, columns), kind)

    smem = pl.BlockSpec(memory_space=pltpu.SMEM)
    params = pltpu.CompilerParams(vmem_limit_bytes=64 << 20)

    near = range(1, count - 1, 2)
    across = [(i, i + 1) for i in near] + [(i + 1, i) for i in near]
    detours = relays(count)
    cut = width

    def column(rows):
        return pl.BlockSpec((rows, cut), lambda j: (0, j))

    pooled_rows = (EDGE_ROWS, RIM_ROWS, TABLE_ROWS, FAR_ROWS, 192, 64, token_rows // 2)
    edge, x1s, i1s, x2s, ys, l4, l1 = pl.pallas_call(
        pool_kernel,
        name="pool",
        grid=(2,),
        out_shape=[shape(rows) for rows in pooled_rows],
        in_specs=[
            smem,
            pl.BlockSpec((token_rows, cut), lambda j: (0, 0)),
            pl.BlockSpec((token_rows, cut), lambda j: (0, 0)),
        ],
        out_specs=[column(rows) for rows in pooled_rows],
        scratch_shapes=[pltpu.VMEM((cut // 128, token_rows, 128), jnp.float32)],
        compiler_params=params,
        cost_estimate=pl.CostEstimate(flops=0, transcendentals=0, bytes_accessed=24 << 20),
    )(me, key_rows, value_rows)

    edge_r = lax.ppermute(edge, "ctx", [(s, detours.get((s, t), t)) for s, t in across])
    x2r = lax.ppermute(
        x2s,
        "ctx",
        [(i, i + 3) for i in range(0, count - 3, 2)] + [(i, i - 3) for i in range(3, count, 2)],
    )
    flow_spans = far_flows(count)
    yrs = [
        lax.ppermute(ys if abs(shifts[0]) == 4 else l4, "ctx", flow_pairs(shifts, count))
        for shifts in flow_spans
    ]
    x1r = lax.ppermute(x1s, "ctx", across)
    mates = [(i, i ^ 1) for i in range(count)]
    i1r = lax.ppermute(i1s, "ctx", mates)

    def head(rows, base=0):
        return pl.BlockSpec((rows, head_size), lambda h, *_: (0, base + h))

    def attention(kernel, name, keys, tables, stats, last=False):
        arrays, specs = [], []
        for table in tables:
            if isinstance(table, tuple):
                arrays += table
                specs += [head(table[0].shape[0])] * 2
            else:
                arrays += [table, table]
                specs += [head(table.shape[0]), head(table.shape[0], HEADS)]
        pairs = token_rows * keys * HEADS
        sums = [shape(token_rows, width, jnp.float32), shape(token_rows, 128, jnp.float32)]
        sum_specs = [head(token_rows), pl.BlockSpec((token_rows, 128), lambda h: (0, 0))]
        return pl.pallas_call(
            kernel,
            name=name,
            grid=(HEADS,),
            out_shape=shape(token_rows, width) if last else sums,
            in_specs=[smem, head(token_rows)] + specs + (sum_specs if stats else []),
            out_specs=head(token_rows) if last else sum_specs,
            scratch_shapes=[pltpu.VMEM((head_size // 128, 128, 128), jnp.float32)] if last else [],
            compiler_params=params,
            cost_estimate=pl.CostEstimate(
                flops=4 * pairs * head_size, transcendentals=pairs, bytes_accessed=12 << 20
            ),
        )(me, query_rows, *arrays, *stats)

    stats = attention(
        near_kernel,
        "near",
        2500,
        [(key_rows, value_rows), l1, i1r],
        (),
    )
    edge_r, stats = lax.optimization_barrier((edge_r, stats))
    via_r = edge_r
    if detours:
        via_r = lax.ppermute(edge_r, "ctx", [(via, t) for (_, t), via in detours.items()])
    x2r, yrs, stats = lax.optimization_barrier((x2r, yrs, stats))
    tables = [x2r, lax.ppermute(x2r, "ctx", mates)]
    for yr in yrs:
        tables += [yr, lax.ppermute(yr, "ctx", mates)]
    edge_r, via_r, x1r, tables = lax.optimization_barrier((edge_r, via_r, x1r, tables))
    xt, i2s = pl.pallas_call(
        functools.partial(rim_kernel, [t for _, t in detours]),
        name="rim",
        grid=(2,),
        out_shape=[shape(TABLE_ROWS), shape(256)],
        in_specs=[smem, column(EDGE_ROWS), column(EDGE_ROWS), column(RIM_ROWS)],
        out_specs=[column(TABLE_ROWS), column(256)],
        scratch_shapes=[pltpu.VMEM((cut // 128, 384, 128), jnp.float32)],
        compiler_params=params,
    )(me, edge_r, via_r, x1r)
    i2r = lax.ppermute(i2s, "ctx", mates)
    kernel = functools.partial(far_kernel, flow_spans, count)
    return attention(kernel, "far", 1088, [xt, i2r] + tables, stats, True)


def solution(mesh):
    spec = P(("dp", "ctx"), None)
    return jax.shard_map(
        on_device, mesh=mesh, in_specs=(spec, spec, spec), out_specs=spec, check_vma=False
    )
```
